32 devices in a mesh: row: 8 (over z, y), col: 4 (over x, core).
Axes of the slice: x: 2, y: 2, z: 4, core: 2. Of those that a mesh axis runs over, the one named last changes fastest.
Arguments:
- trailing: float32 [16384, 16384], P('row', 'col'), may hold values from -40 to 40, as said below
- factor_one: float32 [16384, 512], P(('row', 'col')), may hold values from -0.0390625 to 0.0390625
- inverse_one: float32 [512, 512], replicated, may hold values from -1 to 2, as said below
- factor_two_top: float32 [512, 512], replicated, may hold values from -0.0390625 to 0.0390625
- factor_two: float32 [16384, 512], P(('row', 'col')), may hold values from -0.0390625 to 0.0390625
- inverse_two: float32 [512, 512], replicated, may hold values from -1 to 2, as said below
- structure_one: int32 [96], replicated, may hold values from 0 to 127, as said below
- structure_two: int32 [94], replicated, may hold values from 0 to 127, as said below
Outputs:
- column_one: float32 [16384, 512], P(('row', 'col'))
- diagonal_one: float32 [512, 512], replicated
- column_two: float32 [16384, 512], P(('row', 'col'))
- cross_two: float32 [512, 512], replicated
- diagonal_two: float32 [512, 512], replicated
The draws below stay inside these ranges and needn't reach their ends.
Inputs may be any that keep to these rules, and one draw needn't show every extreme that they name: `trailing`: symmetric. `inverse_one`: lower triangular, diagonal between 1 and 2. `inverse_two`: lower triangular, diagonal between 1 and 2. `structure_one`: distinct, rising; lists block 0 and the last block. `structure_two`: distinct, rising, each also listed in structure_one; lists block 0 and the last block.
All inputs are finite; a program needn't handle non-finite values.
Results may differ from the reference program's by a relative error of at most 0.0003.
Values sent between devices are 32-bit elements; how exact they have to be, the bound alone decides.
A program may use at most 128 MiB of HBM per device.

```python
import math
import jax
import jax.numpy as jnp
from jax import lax

W = 512
BLK = 128
M = 16384
SB1 = 96
SB2 = 94


def draw_trailing(key, part):
    normals = jax.random.truncated_normal(jax.random.fold_in(key, 31), -5.0, 5.0, (M, M), jnp.float32)
    symmetric = (normals + normals.T) * 0.7071067811865476
    places = jnp.arange(M, dtype=jnp.int32)
    return symmetric.at[places, places].add(2.0)


def lower_inverse(key):
    diag_values = jax.random.uniform(jax.random.fold_in(key, 1), (W,), jnp.float32, 1.0, 2.0)
    off_diag = jax.random.truncated_normal(jax.random.fold_in(key, 2), -5.0, 5.0, (W, W), jnp.float32) * (0.8 / math.sqrt(W))
    return jnp.tril(off_diag, -1) + jnp.diag(diag_values)


def draw_inverse_one(key, part):
    return lower_inverse(jax.random.fold_in(key, 11))


def draw_inverse_two(key, part):
    return lower_inverse(jax.random.fold_in(key, 12))


def structure_lists(key):
    count = M // BLK
    inner_blocks = jax.random.permutation(jax.random.fold_in(key, 21), count - 2)[:SB1 - 2].astype(jnp.int32) + 1
    ends = jnp.array([0, count - 1], dtype=jnp.int32)
    first_set = jnp.sort(jnp.concatenate([ends, inner_blocks]))
    chosen = jax.random.permutation(jax.random.fold_in(key, 22), SB1 - 2)[:SB2 - 2]
    second_set = jnp.sort(jnp.concatenate([ends, first_set[1:-1][chosen]]))
    return (first_set, second_set)


def draw_structure_one(key, part):
    return structure_lists(key)[0]


def draw_structure_two(key, part):
    return structure_lists(key)[1]


def shard_levels(key, dims, split, smallest, top_value):
    def one(dim, blocks):
        steps = jax.random.uniform(jax.random.fold_in(jax.random.fold_in(key, 6), dim), (blocks,), jnp.float32, smallest / len(split), top_value / len(split))
        return jnp.repeat(jnp.exp(steps), dims[dim] // blocks).reshape((-1,) + (1,) * (len(dims) - dim - 1))

    level = one(*split[0])
    for cut in split[1:]:
        level = level * one(*cut)
    return level


def centred(own_key, shape, deviation, bound, cuts=(), held_as=jnp.bfloat16):
    drawn = jax.random.normal(own_key, shape, jnp.float32) * deviation
    if len(cuts) > 0:
        drawn = shard_levels(own_key, shape, cuts, -0.22, 0.18) * drawn
    return jnp.clip(drawn, min=-bound, max=bound).astype(held_as)


def setup_inputs(seed: int = 0) -> dict:
    splits = jax.random.split(jax.random.key(seed), 9)
    trailing = draw_trailing(jax.random.fold_in(splits[8], 71), 0)
    factor_one = centred(splits[1], (M, W), (2 * SB1 * BLK) ** -0.5, 0.0390625, ((0, 32),), jnp.float32)
    inverse_one = draw_inverse_one(jax.random.fold_in(splits[8], 71), 0)
    factor_two_top = centred(splits[3], (W, W), (2 * (SB2 * BLK + W)) ** -0.5, 0.0390625, (), jnp.float32)
    factor_two = centred(splits[4], (M, W), (2 * (SB2 * BLK + W)) ** -0.5, 0.0390625, ((0, 32),), jnp.float32)
    inverse_two = draw_inverse_two(jax.random.fold_in(splits[8], 71), 0)
    structure_one = draw_structure_one(jax.random.fold_in(splits[8], 71), 0)
    structure_two = draw_structure_two(jax.random.fold_in(splits[8], 71), 0)
    return {"trailing": trailing, "factor_one": factor_one, "inverse_one": inverse_one, "factor_two_top": factor_two_top, "factor_two": factor_two, "inverse_two": inverse_two, "structure_one": structure_one, "structure_two": structure_two}


def product(left, right):
    return jnp.dot(left, right, precision=lax.Precision.HIGHEST, preferred_element_type=jnp.float32)


def block_flags(structure, count):
    blocks = jnp.arange(count, dtype=jnp.int32) // BLK
    hits = jnp.any(blocks[:, None] == structure[None, :].astype(jnp.int32), axis=1)
    return hits.astype(jnp.float32)[:, None]


def reference(trailing, factor_one, inverse_one, factor_two_top, factor_two, inverse_two, structure_one, structure_two):
    mask_one = block_flags(structure_one, M)
    mask_two = block_flags(structure_two, M)
    normal_one = mask_one * product(factor_one, inverse_one)
    column_one = -mask_one * product(trailing, normal_one)
    diagonal_one = product(inverse_one.T, inverse_one) - product(normal_one.T, column_one)
    normal_top = product(factor_two_top, inverse_two)
    normal_two = mask_two * product(factor_two, inverse_two)
    column_two = -mask_two * (product(column_one, normal_top) + product(trailing, normal_two))
    cross_two = -(product(diagonal_one, normal_top) + product(column_one.T, normal_two))
    diagonal_two = product(inverse_two.T, inverse_two) - product(normal_top.T, cross_two) - product(normal_two.T, column_two)
    return column_one, diagonal_one, column_two, cross_two, diagonal_two
```

```python
import functools

import jax
import jax.numpy as jnp
from jax import lax
from jax.experimental import pallas as pl
from jax.experimental.pallas import tpu as pltpu
from jax.sharding import PartitionSpec as P

BLK = 128
MESH = pl.DeviceIdType.MESH
CH = 8
LAG = 2
RS0 = 9
A0 = 23
F32 = jnp.float32
BF16 = jnp.bfloat16


def product(left, right):
    return jnp.dot(left, right, precision=lax.Precision.HIGHEST, preferred_element_type=jnp.float32)


def big_product(left, right):
    return jnp.dot(left, right, precision=lax.Precision.HIGH, preferred_element_type=jnp.float32)


def block_flags(structure, first_row, count):
    blocks = (first_row + jnp.arange(count, dtype=jnp.int32)) // BLK
    hits = jnp.any(blocks[:, None] == structure[None, :], axis=1)
    return hits.astype(jnp.float32)[:, None]


def split(value):
    high = value.astype(BF16)
    return high, (value - high.astype(F32)).astype(BF16)


def mm(left, right):
    return jnp.dot(left, right, preferred_element_type=F32)


def flip(c, t):
    return ((c // 2 + t // 2) % 2) * 2 + (c % 2 + t % 2) % 2


def panels_kernel(
    trail, n1_in, n2_in, y1_out, y2_out,
    n1buf, n2buf, n2h, n2l, out1, out2, rsu, rsd, rsy, y2buf, tbuf, n1h, n1l, cbuf, xbuf,
    ag_sem, n2_sem, up_sem, dn_sem, ry_sem, y2_sem, t_sem, c_sem, x_sem,
    s_up, s_dn, s_y, s_root, s_n2, s_ry, s_line, s_c, s_x,
):
    r, c = lax.axis_index("row"), lax.axis_index("col")
    z, y, x, k = r // 2, r % 2, c // 2, c % 2
    piece = n1_in.shape[0]
    cr = piece // CH
    wr = n2_in.shape[0] // CH
    ypart = (r + 1 - 2 * y, c)
    cpart = (r, flip(c, 1))
    xpart = (r, flip(c, 2))
    above = (lax.rem(r + 2, 8), c)
    below = (lax.rem(r + 6, 8), c)
    dist = jnp.where(z > c, z - c, c - z)

    def remote(src, dst, send, recv, to):
        return pltpu.make_async_remote_copy(
            src_ref=src, dst_ref=dst, send_sem=send, recv_sem=recv, device_id=to, device_id_type=MESH
        )

    def arrived(ref, sem):
        pltpu.make_async_copy(ref, ref, sem).wait()

    bar = pltpu.get_barrier_semaphore()
    for to in (ypart, cpart, xpart, (r, flip(c, 3))):
        pl.semaphore_signal(bar, inc=1, device_id=to, device_id_type=MESH)

    @pl.when(z < 3)
    def _():
        pl.semaphore_signal(bar, inc=1, device_id=above, device_id_type=MESH)

    @pl.when(z > 0)
    def _():
        pl.semaphore_signal(bar, inc=1, device_id=below, device_id_type=MESH)

    def tile_of(u):
        isa = u // 16
        v = u % 16
        p = v % 8
        tb = (4 - (p + 1) // 2) % 4
        ob = p % 2 + (7 - p) // 7 - p // 7
        hb = (x + v // 8) % 2
        ta, oa, ha = v // 4, (v // 2) % 2, v % 2
        t = isa * ta + (1 - isa) * tb
        o = isa * oa + (1 - isa) * ob
        h = isa * ha + (1 - isa) * hb
        return ((y + o) % 2) * 4 + flip(c, t), h, t, o

    half = 2 * piece

    def fetch(u):
        j, h, _, _ = tile_of(u)
        rows = pl.ds(pl.multiple_of(h * half, half), half)
        cols = pl.ds(pl.multiple_of(j * piece, piece), piece)
        return pltpu.make_async_copy(trail.at[rows, cols], tbuf.at[u % 2], t_sem.at[u % 2])

    fetch(0).start()
    own = pltpu.make_async_copy(n2_in, n2buf.at[c], n2_sem.at[0])
    own.start()

    pl.semaphore_wait(bar, 4 + (z + 2) // 3 + (5 - z) // 3)

    to_x = remote(n2_in, n2buf.at[c], s_n2.at[0], n2_sem.at[2], xpart)
    to_x.start()
    to_c = remote(n2_in, n2buf.at[c], s_n2.at[1], n2_sem.at[1], cpart)
    to_c.start()

    here = y * 4 + c
    for ch in range(CH):
        part = pl.ds(ch * cr, cr)

        @pl.when(c == z)
        def _():
            pltpu.make_async_copy(n1_in.at[part], n1buf.at[here, part], ag_sem.at[here, ch]).start()

        @pl.when(c != z)
        def _():
            remote(n1_in.at[part], n1buf.at[here, part], s_root.at[ch], ag_sem.at[here, ch], (r, z)).start()

    own.wait()
    arrived(n2buf.at[flip(c, 1)], n2_sem.at[1])
    for t in range(2):
        q = flip(c, t)
        n2h[q], n2l[q] = split(n2buf[q])

    def ag_step(n):
        s, ch = n // CH, n % CH
        o = (s + 3) // 4 - (s + 2) // 4
        t = s - (s + 3) // 4
        j = ((y + o) % 2) * 4 + flip(c, t)
        part = pl.ds(pl.multiple_of(ch * cr, cr), cr)
        chunk = n1buf.at[j, part]
        arrived(chunk, ag_sem.at[j, ch])

        @pl.when((z >= c) & (z < 3))
        def _():
            remote(chunk, chunk, s_up.at[n], ag_sem.at[j, ch], above).start()

        @pl.when((z <= c) & (z > 0))
        def _():
            remote(chunk, chunk, s_dn.at[n], ag_sem.at[j, ch], below).start()

        @pl.when((s >= 2) | ((s == 0) & (z == c)))
        def _():
            remote(chunk, chunk, s_y.at[t, ch], ag_sem.at[j, ch], ypart).start()

    def rs_step(n):
        s, ch = n // CH, n % CH
        mine = (s + 3) // 4
        t = (4 - s) * mine
        j = ((y + 1 - mine) % 2) * 4 + flip(c, t)
        part = pl.ds(pl.multiple_of(ch * wr, wr), wr)
        chunk = out2.at[j, part]

        @pl.when((z >= c) & (z < 3))
        def _():
            arrived(rsu.at[s, part], up_sem.at[n])
            chunk[...] += rsu[s, part]

        @pl.when((z <= c) & (z > 0))
        def _():
            arrived(rsd.at[s, part], dn_sem.at[n])
            chunk[...] += rsd[s, part]

        @pl.when(((s >= 1) & (s <= 3)) | ((s == 4) & (z == c)))
        def _():
            arrived(rsy.at[t, part], ry_sem.at[t, ch])
            chunk[...] += rsy[t, part]

        @pl.when(z > c)
        def _():
            remote(chunk, rsu.at[s, part], s_line.at[n], up_sem.at[n], below).start()

        @pl.when(z < c)
        def _():
            remote(chunk, rsd.at[s, part], s_line.at[n], dn_sem.at[n], above).start()

        @pl.when((z == c) & (s == 0))
        def _():
            remote(chunk, rsy.at[0, part], s_line.at[n], ry_sem.at[0, ch], ypart).start()

        @pl.when((z == c) & (s >= 1) & (s <= 3))
        def _():
            remote(chunk, y2buf.at[part], s_line.at[n], y2_sem.at[ch], (r, flip(c, t))).start()

        @pl.when((z == c) & (s == 4))
        def _():
            pltpu.make_async_copy(chunk, y2buf.at[part], y2_sem.at[ch]).start()

    def turn_b(u):
        j, h, t, o = tile_of(u)
        fetch(u).wait()
        fetch(u + 1).start()

        @pl.loop(0, 2)
        def _(i):
            rows = pl.ds(pl.multiple_of(i * piece, piece), piece)
            th, tl = split(tbuf[u % 2, rows])
            q = 2 * h + i
            add = mm(n2h[q], th) + (mm(n2l[q], th) + mm(n2h[q], tl))

            @pl.when((u < 8) & (i == 0))
            def _():
                out2[j] = add

            @pl.when((u >= 8) | (i == 1))
            def _():
                out2[j] += add

        @pl.when((u >= 8) & (o == 1) & (t >= 1))
        def _():
            for ch in range(CH):
                part = pl.ds(ch * wr, wr)
                remote(out2.at[j, part], rsy.at[t, part], s_ry.at[t, ch], ry_sem.at[t, ch], ypart).start()

    def turn_a(u):
        j, h, t, o = tile_of(u)

        @pl.when((h == 0) & (o == 1) & (t >= 1))
        def _():
            for ch in range(CH):
                arrived(n1buf.at[j, pl.ds(ch * cr, cr)], ag_sem.at[j, ch])

        @pl.when(h == 0)
        def _():
            n1h[...], n1l[...] = split(n1buf[j])

        fetch(u).wait()

        @pl.when(u < 31)
        def _():
            fetch(u + 1).start()

        @pl.loop(0, 2)
        def _(i):
            rows = pl.ds(pl.multiple_of(i * piece, piece), piece)
            th, tl = split(tbuf[u % 2, rows])
            add = mm(th, n1h[...]) + (mm(th, n1l[...]) + mm(tl, n1h[...]))
            q = 2 * h + i

            @pl.when(u < 18)
            def _():
                out1[q] = add

            @pl.when(u >= 18)
            def _():
                out1[q] += add

    qx = flip(c, 2)
    end_a = A0 + 28
    ag_first = LAG * dist
    rs_first = RS0 + LAG * jnp.where(z > c, 3 - z, jnp.where(z < c, z, jnp.where(c < 2, 3 - c, c)))

    def core_copy(i):
        to = flip(c, 1 + 2 * (1 - i))
        return remote(out1.at[to], cbuf.at[i], s_c.at[i], c_sem.at[i], cpart)

    x_copy = remote(out1.at[qx], xbuf, s_x.at[0], x_sem.at[0], xpart)

    def tick(step, carry):
        n = step - ag_first

        @pl.when((n >= 0) & (n < 5 * CH))
        def _():
            ag_step(n)

        m = step - rs_first

        @pl.when((m >= 0) & (m < 5 * CH))
        def _():
            rs_step(m)

        @pl.when(step == 8)
        def _():
            got = flip(c, 2)
            arrived(n2buf.at[got], n2_sem.at[2])
            fwd = remote(n2buf.at[got], n2buf.at[got], s_n2.at[2], n2_sem.at[3], cpart)
            fwd.start()
            n2h[got], n2l[got] = split(n2buf[got])
            last = flip(c, 3)
            arrived(n2buf.at[last], n2_sem.at[3])
            n2h[last], n2l[last] = split(n2buf[last])

        @pl.when(step < 16)
        def _():
            turn_b(step)

        w = step - A0

        @pl.when((w >= 0) & (w < 32) & (w % 8 < 4))
        def _():
            turn_a(16 + (w // 8) * 4 + w % 4)

        @pl.when(step == end_a)
        def _():
            core_copy(0).start()
            core_copy(1).start()

        @pl.when(step == end_a + 1)
        def _():
            core_copy(0).wait_recv()
            out1[qx] += cbuf[0]
            x_copy.start()
            core_copy(1).wait_recv()
            out1[c] += cbuf[1]

        return carry

    last_tick = RS0 + 3 * LAG + 5 * CH
    lax.fori_loop(0, max(last_tick, end_a + 2), tick, 0)

    x_copy.wait_recv()
    y1_out[...] = out1[c] + xbuf[...]
    for ch in range(CH):
        part = pl.ds(ch * wr, wr)
        arrived(y2buf.at[part], y2_sem.at[ch])
    y2_out[...] = y2buf[...]

    def sent(ref, sem):
        pltpu.make_async_copy(ref, ref, sem).wait()

    whole = n2buf.at[0]
    for i in range(3):
        sent(whole, s_n2.at[i])
    for i in range(2):
        sent(cbuf.at[0], s_c.at[i])
    sent(xbuf, s_x.at[0])
    bit = n1buf.at[0, pl.ds(0, cr)]
    wbit = out2.at[0, pl.ds(0, wr)]

    @pl.loop(0, 5 * CH)
    def _(n):
        s, ch = n // CH, n % CH

        @pl.when((z >= c) & (z < 3))
        def _():
            sent(bit, s_up.at[n])

        @pl.when((z <= c) & (z > 0))
        def _():
            sent(bit, s_dn.at[n])

        @pl.when((s >= 2) | ((s == 0) & (z == c)))
        def _():
            sent(bit, s_y.at[s - (s + 3) // 4, ch])

        @pl.when((z != c) | (s < 4))
        def _():
            sent(wbit, s_line.at[n])

        @pl.when((s >= 1) & (s <= 3))
        def _():
            sent(wbit, s_ry.at[s, ch])

        @pl.when((s == 0) & (c != z))
        def _():
            sent(bit, s_root.at[ch])


def panels(trailing, n1, n2t):
    piece, width = n1.shape
    dma = pltpu.SemaphoreType.DMA
    vm = pltpu.VMEM
    scratch = [
        vm((8, piece, width), F32),
        vm((4, width, piece), F32),
        vm((4, width, piece), BF16),
        vm((4, width, piece), BF16),
        vm((4, piece, width), F32),
        vm((8, width, piece), F32),
        vm((5, width, piece), F32),
        vm((5, width, piece), F32),
        vm((4, width, piece), F32),
        vm((width, piece), F32),
        vm((2, 2 * piece, piece), F32),
        vm((piece, width), BF16),
        vm((piece, width), BF16),
        vm((2, piece, width), F32),
        vm((piece, width), F32),
        dma((8, CH)), dma((4,)), dma((5 * CH,)), dma((5 * CH,)), dma((4, CH)), dma((CH,)), dma((2,)), dma((2,)), dma((1,)),
        dma((5 * CH,)), dma((5 * CH,)), dma((4, CH)), dma((CH,)), dma((3,)), dma((4, CH)), dma((5 * CH,)), dma((2,)), dma((1,)),
    ]
    anyspace = pl.BlockSpec(memory_space=pl.ANY)
    inv = pl.BlockSpec(memory_space=pltpu.VMEM)
    return pl.pallas_call(
        panels_kernel,
        out_shape=(
            jax.ShapeDtypeStruct((piece, width), F32),
            jax.ShapeDtypeStruct((width, piece), F32),
        ),
        in_specs=[anyspace, anyspace, anyspace],
        out_specs=(inv, inv),
        scratch_shapes=scratch,
        compiler_params=pltpu.CompilerParams(
            collective_id=0, has_side_effects=True, vmem_limit_bytes=63 * 2**20
        ),
        name="panels",
    )(trailing, n1, n2t)


def column_panel(normal):
    rows, cols = lax.axis_size("row"), lax.axis_size("col")
    moves = [(p, (p % rows) * cols + p // rows) for p in range(rows * cols)]
    piece = lax.ppermute(normal, ("row", "col"), moves)
    return lax.all_gather(piece, "row", axis=0, tiled=True)


def total_over_all(x):
    return lax.psum(x, ("row", "col"))


def sweep(trailing, col_block):
    part = big_product(trailing, col_block)
    return lax.psum_scatter(part, "col", scatter_dimension=0, tiled=True)


def body(
    special,
    trailing,
    factor_one,
    inverse_one,
    factor_two_top,
    factor_two,
    inverse_two,
    structure_one,
    structure_two,
):
    piece_rows = factor_one.shape[0]
    row_index = lax.axis_index("row")
    col_index = lax.axis_index("col")
    first_row = (row_index * lax.axis_size("col") + col_index) * piece_rows
    mask_one = block_flags(structure_one, first_row, piece_rows)
    mask_two = block_flags(structure_two, first_row, piece_rows)
    normal_one = mask_one * product(factor_one, inverse_one)
    normal_two = mask_two * product(factor_two, inverse_two)
    normal_top = product(factor_two_top, inverse_two)
    if special:
        sum_one, sum_two = panels(trailing, normal_one, normal_two.T)
        sum_two = sum_two.T
    else:
        sum_one = sweep(trailing, column_panel(normal_one))
        sum_two = sweep(trailing, column_panel(normal_two))
    column_one = -mask_one * sum_one
    both = product(column_one.T, jnp.concatenate([normal_one, normal_two], axis=1))
    column_two = -mask_two * (sum_two + product(column_one, normal_top))
    second = product(normal_two.T, column_two)
    totals = total_over_all(jnp.concatenate([both, second], axis=1))
    width = normal_one.shape[1]
    diagonal_one = product(inverse_one.T, inverse_one) - totals[:, :width].T
    cross_two = -(product(diagonal_one, normal_top) + totals[:, width : 2 * width])
    diagonal_two = (
        product(inverse_two.T, inverse_two)
        - product(normal_top.T, cross_two)
        - totals[:, 2 * width :]
    )
    return (column_one, diagonal_one, column_two, cross_two, diagonal_two)


def solution(mesh):
    special = mesh.shape["row"] == 8 and mesh.shape["col"] == 4
    return jax.shard_map(
        functools.partial(body, special),
        mesh=mesh,
        in_specs=(
            P("row", "col"),
            P(("row", "col"), None),
            P(),
            P(),
            P(("row", "col"), None),
            P(),
            P(),
            P(),
        ),
        out_specs=(P(("row", "col"), None), P(), P(("row", "col"), None), P(), P()),
        check_vma=False,
    )
```

```python
import functools

import jax
import jax.numpy as jnp
from jax import lax
from jax.experimental import pallas as pl
from jax.experimental.pallas import tpu as pltpu
from jax.sharding import PartitionSpec as P

BLK = 128
MESH = pl.DeviceIdType.MESH
CH = 8
LAG = 2
RS0 = 9
A0 = 23
F32 = jnp.float32
BF16 = jnp.bfloat16


def product(left, right):
    return jnp.dot(left, right, precision=lax.Precision.HIGHEST, preferred_element_type=jnp.float32)


def big_product(left, right):
    return jnp.dot(left, right, precision=lax.Precision.HIGH, preferred_element_type=jnp.float32)


def block_flags(structure, first_row, count):
    blocks = (first_row + jnp.arange(count, dtype=jnp.int32)) // BLK
    hits = jnp.any(blocks[:, None] == structure[None, :], axis=1)
    return hits.astype(jnp.float32)[:, None]


def split(value):
    high = value.astype(BF16)
    return high, (value - high.astype(F32)).astype(BF16)


def mm(left, right):
    return jnp.dot(left, right, preferred_element_type=F32)


def flip(c, t):
    return ((c // 2 + t // 2) % 2) * 2 + (c % 2 + t % 2) % 2


def panels_kernel(
    trail, n1_in, n2_in, y1_out, y2_out,
    n1buf, n2buf, n2h, n2l, out1, out2, rsu, rsd, rsy, y2buf, tbuf, n1h, n1l, cbuf, xbuf,
    ag_sem, n2_sem, up_sem, dn_sem, ry_sem, y2_sem, t_sem, c_sem, x_sem,
    s_up, s_dn, s_y, s_root, s_n2, s_ry, s_line, s_c, s_x,
):
    r, c = lax.axis_index("row"), lax.axis_index("col")
    z, y, x, k = r // 2, r % 2, c // 2, c % 2
    piece = n1_in.shape[0]
    cr = piece // CH
    wr = n2_in.shape[0] // CH
    ypart = (r + 1 - 2 * y, c)
    cpart = (r, flip(c, 1))
    xpart = (r, flip(c, 2))
    above = (lax.rem(r + 2, 8), c)
    below = (lax.rem(r + 6, 8), c)
    dist = jnp.where(z > c, z - c, c - z)

    def remote(src, dst, send, recv, to):
        return pltpu.make_async_remote_copy(
            src_ref=src, dst_ref=dst, send_sem=send, recv_sem=recv, device_id=to, device_id_type=MESH
        )

    def arrived(ref, sem):
        pltpu.make_async_copy(ref, ref, sem).wait()

    bar = pltpu.get_barrier_semaphore()
    for to in (ypart, cpart, xpart, (r, flip(c, 3))):
        pl.semaphore_signal(bar, inc=1, device_id=to, device_id_type=MESH)

    @pl.when(z < 3)
    def _():
        pl.semaphore_signal(bar, inc=1, device_id=above, device_id_type=MESH)

    @pl.when(z > 0)
    def _():
        pl.semaphore_signal(bar, inc=1, device_id=below, device_id_type=MESH)

    def tile_of(u):
        isa = u // 16
        v = u % 16
        p = v % 8
        tb = (4 - (p + 1) // 2) % 4
        ob = p % 2 + (7 - p) // 7 - p // 7
        hb = (x + v // 8) % 2
        ta, oa, ha = v // 4, (v // 2) % 2, v % 2
        t = isa * ta + (1 - isa) * tb
        o = isa * oa + (1 - isa) * ob
        h = isa * ha + (1 - isa) * hb
        return ((y + o) % 2) * 4 + flip(c, t), h, t, o

    half = 2 * piece

    def fetch(u):
        j, h, _, _ = tile_of(u)
        rows = pl.ds(pl.multiple_of(h * half, half), half)
        cols = pl.ds(pl.multiple_of(j * piece, piece), piece)
        return pltpu.make_async_copy(trail.at[rows, cols], tbuf.at[u % 2], t_sem.at[u % 2])

    fetch(0).start()
    own = pltpu.make_async_copy(n2_in, n2buf.at[c], n2_sem.at[0])
    own.start()

    pl.semaphore_wait(bar, 4 + (z + 2) // 3 + (5 - z) // 3)

    to_x = remote(n2_in, n2buf.at[c], s_n2.at[0], n2_sem.at[2], xpart)
    to_x.start()
    to_c = remote(n2_in, n2buf.at[c], s_n2.at[1], n2_sem.at[1], cpart)
    to_c.start()

    here = y * 4 + c
    for ch in range(CH):
        part = pl.ds(ch * cr, cr)

        @pl.when(c == z)
        def _():
            pltpu.make_async_copy(n1_in.at[part], n1buf.at[here, part], ag_sem.at[here, ch]).start()

        @pl.when(c != z)
        def _():
            remote(n1_in.at[part], n1buf.at[here, part], s_root.at[ch], ag_sem.at[here, ch], (r, z)).start()

    own.wait()
    arrived(n2buf.at[flip(c, 1)], n2_sem.at[1])
    for t in range(2):
        q = flip(c, t)
        n2h[q], n2l[q] = split(n2buf[q])

    def ag_step(n):
        s, ch = n // CH, n % CH
        o = (s + 3) // 4 - (s + 2) // 4
        t = s - (s + 3) // 4
        j = ((y + o) % 2) * 4 + flip(c, t)
        part = pl.ds(pl.multiple_of(ch * cr, cr), cr)
        chunk = n1buf.at[j, part]
        arrived(chunk, ag_sem.at[j, ch])

        @pl.when((z >= c) & (z < 3))
        def _():
            remote(chunk, chunk, s_up.at[n], ag_sem.at[j, ch], above).start()

        @pl.when((z <= c) & (z > 0))
        def _():
            remote(chunk, chunk, s_dn.at[n], ag_sem.at[j, ch], below).start()

        @pl.when((s >= 2) | ((s == 0) & (z == c)))
        def _():
            remote(chunk, chunk, s_y.at[t, ch], ag_sem.at[j, ch], ypart).start()

    def rs_step(n):
        s, ch = n // CH, n % CH
        mine = (s + 3) // 4
        t = (4 - s) * mine
        j = ((y + 1 - mine) % 2) * 4 + flip(c, t)
        part = pl.ds(pl.multiple_of(ch * wr, wr), wr)
        chunk = out2.at[j, part]

        @pl.when((z >= c) & (z < 3))
        def _():
            arrived(rsu.at[s, part], up_sem.at[n])
            chunk[...] += rsu[s, part]

        @pl.when((z <= c) & (z > 0))
        def _():
            arrived(rsd.at[s, part], dn_sem.at[n])
            chunk[...] += rsd[s, part]

        @pl.when(((s >= 1) & (s <= 3)) | ((s == 4) & (z == c)))
        def _():
            arrived(rsy.at[t, part], ry_sem.at[t, ch])
            chunk[...] += rsy[t, part]

        @pl.when(z > c)
        def _():
            remote(chunk, rsu.at[s, part], s_line.at[n], up_sem.at[n], below).start()

        @pl.when(z < c)
        def _():
            remote(chunk, rsd.at[s, part], s_line.at[n], dn_sem.at[n], above).start()

        @pl.when((z == c) & (s == 0))
        def _():
            remote(chunk, rsy.at[0, part], s_line.at[n], ry_sem.at[0, ch], ypart).start()

        @pl.when((z == c) & (s >= 1) & (s <= 3))
        def _():
            remote(chunk, y2buf.at[part], s_line.at[n], y2_sem.at[ch], (r, flip(c, t))).start()

        @pl.when((z == c) & (s == 4))
        def _():
            pltpu.make_async_copy(chunk, y2buf.at[part], y2_sem.at[ch]).start()

    def turn_b(u):
        j, h, t, o = tile_of(u)
        fetch(u).wait()
        fetch(u + 1).start()

        @pl.loop(0, 2)
        def _(i):
            rows = pl.ds(pl.multiple_of(i * piece, piece), piece)
            th, tl = split(tbuf[u % 2, rows])
            q = 2 * h + i
            add = mm(n2h[q], th) + (mm(n2l[q], th) + mm(n2h[q], tl))

            @pl.when((u < 8) & (i == 0))
            def _():
                out2[j] = add

            @pl.when((u >= 8) | (i == 1))
            def _():
                out2[j] += add

        @pl.when((u >= 8) & (o == 1) & (t >= 1))
        def _():
            for ch in range(CH):
                part = pl.ds(ch * wr, wr)
                remote(out2.at[j, part], rsy.at[t, part], s_ry.at[t, ch], ry_sem.at[t, ch], ypart).start()

    def turn_a(u):
        j, h, t, o = tile_of(u)

        @pl.when((h == 0) & (o == 1) & (t >= 1))
        def _():
            for ch in range(CH):
                arrived(n1buf.at[j, pl.ds(ch * cr, cr)], ag_sem.at[j, ch])

        @pl.when(h == 0)
        def _():
            n1h[...], n1l[...] = split(n1buf[j])

        fetch(u).wait()

        @pl.when(u < 31)
        def _():
            fetch(u + 1).start()

        @pl.loop(0, 2)
        def _(i):
            rows = pl.ds(pl.multiple_of(i * piece, piece), piece)
            th, tl = split(tbuf[u % 2, rows])
            add = mm(th, n1h[...]) + (mm(th, n1l[...]) + mm(tl, n1h[...]))
            q = 2 * h + i

            @pl.when(u < 18)
            def _():
                out1[q] = add

            @pl.when(u >= 18)
            def _():
                out1[q] += add

    qx = flip(c, 2)
    end_a = A0 + 28
    ag_first = LAG * dist
    rs_first = RS0 + LAG * jnp.where(z > c, 3 - z, jnp.where(z < c, z, jnp.where(c < 2, 3 - c, c)))

    def core_copy(i):
        to = flip(c, 1 + 2 * (1 - i))
        return remote(out1.at[to], cbuf.at[i], s_c.at[i], c_sem.at[i], cpart)

    x_copy = remote(out1.at[qx], xbuf, s_x.at[0], x_sem.at[0], xpart)

    def tick(step, carry):
        n = step - ag_first

        @pl.when((n >= 0) & (n < 5 * CH))
        def _():
            ag_step(n)

        m = step - rs_first

        @pl.when((m >= 0) & (m < 5 * CH))
        def _():
            rs_step(m)

        @pl.when(step == 8)
        def _():
            got = flip(c, 2)
            arrived(n2buf.at[got], n2_sem.at[2])
            fwd = remote(n2buf.at[got], n2buf.at[got], s_n2.at[2], n2_sem.at[3], cpart)
            fwd.start()
            n2h[got], n2l[got] = split(n2buf[got])
            last = flip(c, 3)
            arrived(n2buf.at[last], n2_sem.at[3])
            n2h[last], n2l[last] = split(n2buf[last])

        @pl.when(step < 16)
        def _():
            turn_b(step)

        w = step - A0

        @pl.when((w >= 0) & (w < 32) & (w % 8 < 4))
        def _():
            turn_a(16 + (w // 8) * 4 + w % 4)

        @pl.when(step == end_a)
        def _():
            core_copy(0).start()
            core_copy(1).start()

        @pl.when(step == end_a + 1)
        def _():
            core_copy(0).wait_recv()
            out1[qx] += cbuf[0]
            x_copy.start()
            core_copy(1).wait_recv()
            out1[c] += cbuf[1]

        return carry

    last_tick = RS0 + 3 * LAG + 5 * CH
    lax.fori_loop(0, max(last_tick, end_a + 2), tick, 0)

    x_copy.wait_recv()
    y1_out[...] = out1[c] + xbuf[...]
    for ch in range(CH):
        part = pl.ds(ch * wr, wr)
        arrived(y2buf.at[part], y2_sem.at[ch])
    y2_out[...] = y2buf[...]

    def sent(ref, sem):
        pltpu.make_async_copy(ref, ref, sem).wait()

    whole = n2buf.at[0]
    for i in range(3):
        sent(whole, s_n2.at[i])
    for i in range(2):
        sent(cbuf.at[0], s_c.at[i])
    sent(xbuf, s_x.at[0])
    bit = n1buf.at[0, pl.ds(0, cr)]
    wbit = out2.at[0, pl.ds(0, wr)]

    @pl.loop(0, 5 * CH)
    def _(n):
        s, ch = n // CH, n % CH

        @pl.when((z >= c) & (z < 3))
        def _():
            sent(bit, s_up.at[n])

        @pl.when((z <= c) & (z > 0))
        def _():
            sent(bit, s_dn.at[n])

        @pl.when((s >= 2) | ((s == 0) & (z == c)))
        def _():
            sent(bit, s_y.at[s - (s + 3) // 4, ch])

        @pl.when((z != c) | (s < 4))
        def _():
            sent(wbit, s_line.at[n])

        @pl.when((s >= 1) & (s <= 3))
        def _():
            sent(wbit, s_ry.at[s, ch])

        @pl.when((s == 0) & (c != z))
        def _():
            sent(bit, s_root.at[ch])


def panels(trailing, n1, n2t):
    piece, width = n1.shape
    dma = pltpu.SemaphoreType.DMA
    vm = pltpu.VMEM
    scratch = [
        vm((8, piece, width), F32),
        vm((4, width, piece), F32),
        vm((4, width, piece), BF16),
        vm((4, width, piece), BF16),
        vm((4, piece, width), F32),
        vm((8, width, piece), F32),
        vm((5, width, piece), F32),
        vm((5, width, piece), F32),
        vm((4, width, piece), F32),
        vm((width, piece), F32),
        vm((2, 2 * piece, piece), F32),
        vm((piece, width), BF16),
        vm((piece, width), BF16),
        vm((2, piece, width), F32),
        vm((piece, width), F32),
        dma((8, CH)), dma((4,)), dma((5 * CH,)), dma((5 * CH,)), dma((4, CH)), dma((CH,)), dma((2,)), dma((2,)), dma((1,)),
        dma((5 * CH,)), dma((5 * CH,)), dma((4, CH)), dma((CH,)), dma((3,)), dma((4, CH)), dma((5 * CH,)), dma((2,)), dma((1,)),
    ]
    anyspace = pl.BlockSpec(memory_space=pl.ANY)
    inv = pl.BlockSpec(memory_space=pltpu.VMEM)
    return pl.pallas_call(
        panels_kernel,
        out_shape=(
            jax.ShapeDtypeStruct((piece, width), F32),
            jax.ShapeDtypeStruct((width, piece), F32),
        ),
        in_specs=[anyspace, anyspace, anyspace],
        out_specs=(inv, inv),
        scratch_shapes=scratch,
        compiler_params=pltpu.CompilerParams(
            collective_id=0, has_side_effects=True, vmem_limit_bytes=63 * 2**20
        ),
        name="panels",
    )(trailing, n1, n2t)


def total_kernel(s_in, out, acc, got1, got2, got3, got4, sem1, sem2, sem3, sem4, sem5, sem6, sem7, sem8, s_sem, z_send, z_send2):
    r, c = lax.axis_index("row"), lax.axis_index("col")
    z, y, x, k = r // 2, r % 2, c // 2, c % 2
    ypart = (r + 1 - 2 * y, c)
    cpart = (r, flip(c, 1))
    xpart = (r, flip(c, 2))
    rows = s_in.shape[1]
    h1, h2, h3, h4 = rows // 2, rows // 4, rows // 8, rows // 32

    def remote(src, dst, send, recv, to):
        return pltpu.make_async_remote_copy(
            src_ref=src, dst_ref=dst, send_sem=send, recv_sem=recv, device_id=to, device_id_type=MESH
        )

    def span(start, size):
        return pl.ds(pl.multiple_of(start, size), size)

    bar = pltpu.get_barrier_semaphore()
    line = [(lax.rem(r + 2 * d, 8), c) for d in (1, 2, 3)]
    for to in [ypart, cpart, xpart] + line:
        pl.semaphore_signal(bar, inc=1, device_id=to, device_id_type=MESH)
    pl.semaphore_wait(bar, 6)

    sends = []

    def exchange(pairs):
        copies = [remote(*p) for p in pairs]
        for cp in copies:
            cp.start()
        for cp in copies:
            cp.wait_recv()
        sends.extend(copies)

    base = k * h1
    exchange([(s_in.at[i, span((1 - k) * h1, h1)], got1.at[i], s_sem.at[0, i], sem1.at[i], cpart) for i in (0, 1)])
    for i in (0, 1):
        acc[i] = s_in[i, span(base, h1)] + got1[i]
    first = (x, y)
    second = (y, x)
    one = (xpart, ypart)
    two = (ypart, xpart)
    exchange([(acc.at[i, span((1 - first[i]) * h2, h2)], got2.at[i], s_sem.at[1, i], sem2.at[i], one[i]) for i in (0, 1)])
    at1 = [first[i] * h2 for i in (0, 1)]
    for i in (0, 1):
        acc[i, span(at1[i], h2)] += got2[i]
    exchange(
        [
            (acc.at[i, span(at1[i] + (1 - second[i]) * h3, h3)], got3.at[i], s_sem.at[2, i], sem3.at[i], two[i])
            for i in (0, 1)
        ]
    )
    at2 = [at1[i] + second[i] * h3 for i in (0, 1)]
    for i in (0, 1):
        acc[i, span(at2[i], h3)] += got3[i]
    pairs = []
    for d in (1, 2, 3):
        to_z = lax.rem(z + d, 4)
        for i in (0, 1):
            pairs.append(
                (acc.at[i, span(at2[i] + to_z * h4, h4)], got4.at[d - 1, i], z_send.at[d - 1, i], sem4.at[d - 1, i], line[d - 1])
            )
    exchange(pairs)
    pairs = []
    for i in (0, 1):
        mine = acc[i, span(at2[i] + z * h4, h4)] + got4[0, i] + (got4[1, i] + got4[2, i])
        place = span(base + at2[i] + z * h4, h4)
        out[i, place] = mine
    for d in (1, 2, 3):
        for i in (0, 1):
            place = span(base + at2[i] + z * h4, h4)
            pairs.append((out.at[i, place], out.at[i, place], z_send2.at[d - 1, i], sem5.at[d - 1, i], line[d - 1]))
    exchange(pairs)
    places = [span(base + at2[i], h3) for i in (0, 1)]
    exchange([(out.at[i, places[i]], out.at[i, places[i]], s_sem.at[3, i], sem6.at[i], two[i]) for i in (0, 1)])
    places = [span(base + at1[i], h2) for i in (0, 1)]
    exchange([(out.at[i, places[i]], out.at[i, places[i]], s_sem.at[4, i], sem7.at[i], one[i]) for i in (0, 1)])
    place = span(base, h1)
    exchange([(out.at[i, place], out.at[i, place], s_sem.at[5, i], sem8.at[i], cpart) for i in (0, 1)])
    for cp in sends:
        cp.wait_send()


def total_special(x):
    rows, cols = x.shape
    stacked = jnp.stack([x[:, : cols // 2], x[:, cols // 2 :]])
    w = cols // 2
    dma = pltpu.SemaphoreType.DMA
    vm = pltpu.VMEM
    inv = pl.BlockSpec(memory_space=pltpu.VMEM)
    out = pl.pallas_call(
        total_kernel,
        out_shape=jax.ShapeDtypeStruct((2, rows, w), F32),
        in_specs=[inv],
        out_specs=inv,
        scratch_shapes=[
            vm((2, rows // 2, w), F32),
            vm((2, rows // 2, w), F32),
            vm((2, rows // 4, w), F32),
            vm((2, rows // 8, w), F32),
            vm((3, 2, rows // 32, w), F32),
            dma((2,)), dma((2,)), dma((2,)), dma((3, 2)), dma((3, 2)), dma((2,)), dma((2,)), dma((2,)),
            dma((6, 2)), dma((3, 2)), dma((3, 2)),
        ],
        compiler_params=pltpu.CompilerParams(
            collective_id=1, has_side_effects=True, vmem_limit_bytes=40 * 2**20
        ),
        name="total",
    )(stacked)
    return jnp.concatenate([out[0], out[1]], axis=1)


def column_panel(normal):
    rows, cols = lax.axis_size("row"), lax.axis_size("col")
    moves = [(p, (p % rows) * cols + p // rows) for p in range(rows * cols)]
    piece = lax.ppermute(normal, ("row", "col"), moves)
    return lax.all_gather(piece, "row", axis=0, tiled=True)


def total_over_all(x):
    return lax.psum(x, ("row", "col"))


def sweep(trailing, col_block):
    part = big_product(trailing, col_block)
    return lax.psum_scatter(part, "col", scatter_dimension=0, tiled=True)


def body(
    special,
    trailing,
    factor_one,
    inverse_one,
    factor_two_top,
    factor_two,
    inverse_two,
    structure_one,
    structure_two,
):
    piece_rows = factor_one.shape[0]
    row_index = lax.axis_index("row")
    col_index = lax.axis_index("col")
    first_row = (row_index * lax.axis_size("col") + col_index) * piece_rows
    mask_one = block_flags(structure_one, first_row, piece_rows)
    mask_two = block_flags(structure_two, first_row, piece_rows)
    normal_one = mask_one * product(factor_one, inverse_one)
    normal_two = mask_two * product(factor_two, inverse_two)
    normal_top = product(factor_two_top, inverse_two)
    if special:
        sum_one, sum_two = panels(trailing, normal_one, normal_two.T)
        sum_two = sum_two.T
    else:
        sum_one = sweep(trailing, column_panel(normal_one))
        sum_two = sweep(trailing, column_panel(normal_two))
    column_one = -mask_one * sum_one
    both = product(column_one.T, jnp.concatenate([normal_one, normal_two], axis=1))
    column_two = -mask_two * (sum_two + product(column_one, normal_top))
    second = product(normal_two.T, column_two)
    totals = (total_special if special else total_over_all)(jnp.concatenate([both, second], axis=1))
    width = normal_one.shape[1]
    diagonal_one = product(inverse_one.T, inverse_one) - totals[:, :width].T
    cross_two = -(product(diagonal_one, normal_top) + totals[:, width : 2 * width])
    diagonal_two = (
        product(inverse_two.T, inverse_two)
        - product(normal_top.T, cross_two)
        - totals[:, 2 * width :]
    )
    return (column_one, diagonal_one, column_two, cross_two, diagonal_two)


def solution(mesh):
    special = mesh.shape["row"] == 8 and mesh.shape["col"] == 4
    return jax.shard_map(
        functools.partial(body, special),
        mesh=mesh,
        in_specs=(
            P("row", "col"),
            P(("row", "col"), None),
            P(),
            P(),
            P(("row", "col"), None),
            P(),
            P(),
            P(),
        ),
        out_specs=(P(("row", "col"), None), P(), P(("row", "col"), None), P(), P()),
        check_vma=False,
    )
```

```python
import functools

import jax
import jax.numpy as jnp
from jax import lax
from jax.experimental import pallas as pl
from jax.experimental.pallas import tpu as pltpu
from jax.sharding import PartitionSpec as P

BLK = 128
MESH = pl.DeviceIdType.MESH
CH = 8
AG_LAG = 1
RS_LAG = 4
RS0 = 10
Y0 = 9
Y_RATE = 2
ROOT_RATE = 2
AG_O, AG_T = (0, 0, 0, 0, 1), (1, 0, 2, 3, 0)
RS_O, RS_T = (1, 0, 0, 0, 0), (0, 3, 2, 1, 0)
B_O, B_T = (1, 1, 0, 1, 0, 1, 0, 0), (0, 3, 3, 2, 2, 1, 1, 0)
A_O, A_T = (0, 0, 1, 0, 0, 1, 1, 1), (1, 0, 1, 2, 3, 2, 0, 3)
Y_T = (3, 2, 1)
A_TICK = (16, 17, 19, 20, 21, 22, 27, 28, 35, 36, 37, 38, 43, 44, 45, 46)
F32 = jnp.float32
BF16 = jnp.bfloat16


def product(left, right):
    return jnp.dot(left, right, precision=lax.Precision.HIGHEST, preferred_element_type=jnp.float32)


def big_product(left, right):
    return jnp.dot(left, right, precision=lax.Precision.HIGH, preferred_element_type=jnp.float32)


def block_flags(structure, first_row, count):
    blocks = (first_row + jnp.arange(count, dtype=jnp.int32)) // BLK
    hits = jnp.any(blocks[:, None] == structure[None, :], axis=1)
    return hits.astype(jnp.float32)[:, None]


def split(value):
    high = value.astype(BF16)
    return high, (value - high.astype(F32)).astype(BF16)


def mm(left, right):
    return jnp.dot(left, right, preferred_element_type=F32)


def mm3(left, right):
    lh, ll = split(left)
    rh, rl = split(right)
    return mm(lh, rh) + (mm(ll, rh) + mm(lh, rl))


def flip(c, t):
    return ((c // 2 + t // 2) % 2) * 2 + (c % 2 + t % 2) % 2


def pick(table, index):
    return sum(jnp.where(index == i, v, 0) for i, v in enumerate(table) if v)


def panels_kernel(
    trail, f1, inv1, f2, inv2, mask1, mask2, y1_out, y2_out, n1_in, n2_in,
    n1buf, n2buf, n2h, n2l, out1, out2, rsu, rsd, rsy, y2buf, tbuf, n1h, n1l, cbuf, xbuf,
    f_sem, ag_sem, n2_sem, up_sem, dn_sem, ry_sem, y2_sem, t_sem, c_sem, x_sem,
    s_up, s_dn, s_y, s_root, s_n2, s_ry, s_line, s_c, s_x,
):
    r, c = lax.axis_index("row"), lax.axis_index("col")
    z, y, x, k = r // 2, r % 2, c // 2, c % 2
    piece = n1_in.shape[0]
    cr = piece // CH
    wr = n2_in.shape[0] // CH
    ypart = (r + 1 - 2 * y, c)
    cpart = (r, flip(c, 1))
    xpart = (r, flip(c, 2))
    above = (lax.rem(r + 2, 8), c)
    below = (lax.rem(r + 6, 8), c)
    dist = jnp.where(z > c, z - c, c - z)

    def remote(src, dst, send, recv, to):
        return pltpu.make_async_remote_copy(
            src_ref=src, dst_ref=dst, send_sem=send, recv_sem=recv, device_id=to, device_id_type=MESH
        )

    def arrived(ref, sem):
        pltpu.make_async_copy(ref, ref, sem).wait()

    bar = pltpu.get_barrier_semaphore()
    for to in (ypart, cpart, xpart, (r, flip(c, 3))):
        pl.semaphore_signal(bar, inc=1, device_id=to, device_id_type=MESH)

    @pl.when(z < 3)
    def _():
        pl.semaphore_signal(bar, inc=1, device_id=above, device_id_type=MESH)

    @pl.when(z > 0)
    def _():
        pl.semaphore_signal(bar, inc=1, device_id=below, device_id_type=MESH)

    def tile_of(u):
        isa = u // 16
        v = u % 16
        hb, ha = (x + v // 8) % 2, v % 2
        pb, pa = v % 8, v // 2
        t = isa * pick(A_T, pa) + (1 - isa) * pick(B_T, pb)
        o = isa * pick(A_O, pa) + (1 - isa) * pick(B_O, pb)
        h = isa * ha + (1 - isa) * hb
        return ((y + o) % 2) * 4 + flip(c, t), h, t, o

    half = 2 * piece

    def fetch(u):
        j, h, _, _ = tile_of(u)
        rows = pl.ds(pl.multiple_of(h * half, half), half)
        cols = pl.ds(pl.multiple_of(j * piece, piece), piece)
        return pltpu.make_async_copy(trail.at[rows, cols], tbuf.at[u % 2], t_sem.at[u % 2])

    fetch(0).start()
    loads = [pltpu.make_async_copy(a, out2.at[i], f_sem.at[i]) for i, a in enumerate((f2, inv2, f1, inv1))]
    for cp in loads:
        cp.start()
    loads[0].wait()
    loads[1].wait()
    n2_in[...] = (mask2[...] * mm3(out2[0], out2[1])).T
    own = pltpu.make_async_copy(n2_in, n2buf.at[c], n2_sem.at[0])
    own.start()

    pl.semaphore_wait(bar, 4 + (z + 2) // 3 + (5 - z) // 3)

    to_x = remote(n2_in, n2buf.at[c], s_n2.at[0], n2_sem.at[2], xpart)
    to_x.start()
    to_c = remote(n2_in, n2buf.at[c], s_n2.at[1], n2_sem.at[1], cpart)
    to_c.start()

    loads[2].wait()
    loads[3].wait()
    n1_in[...] = mask1[...] * mm3(out2[2], out2[3])
    here = y * 4 + c
    for ch in range(CH):
        part = pl.ds(ch * cr, cr)

        @pl.when(c == z)
        def _():
            pltpu.make_async_copy(n1_in.at[part], n1buf.at[here, part], ag_sem.at[here, ch]).start()

        @pl.when(c != z)
        def _():
            remote(n1_in.at[part], n1buf.at[here, part], s_root.at[ch], ag_sem.at[here, ch], (r, z)).start()

    own.wait()
    arrived(n2buf.at[flip(c, 1)], n2_sem.at[1])
    for t in range(2):
        q = flip(c, t)
        n2h[q], n2l[q] = split(n2buf[q])

    def ag_step(n):
        s, ch = n // CH, n % CH
        o, t = pick(AG_O, s), pick(AG_T, s)
        j = ((y + o) % 2) * 4 + flip(c, t)
        part = pl.ds(pl.multiple_of(ch * cr, cr), cr)
        chunk = n1buf.at[j, part]
        arrived(chunk, ag_sem.at[j, ch])

        @pl.when((z >= c) & (z < 3))
        def _():
            remote(chunk, chunk, s_up.at[n], ag_sem.at[j, ch], above).start()

        @pl.when((z <= c) & (z > 0))
        def _():
            remote(chunk, chunk, s_dn.at[n], ag_sem.at[j, ch], below).start()

        @pl.when((o == 0) & ((t > 0) | (z == c)))
        def _():
            remote(chunk, chunk, s_y.at[t, ch], ag_sem.at[j, ch], ypart).start()

    def rs_step(n):
        s, ch = n // CH, n % CH
        o, t = pick(RS_O, s), pick(RS_T, s)
        j = ((y + o) % 2) * 4 + flip(c, t)
        part = pl.ds(pl.multiple_of(ch * wr, wr), wr)
        chunk = out2.at[j, part]

        @pl.when((z >= c) & (z < 3))
        def _():
            arrived(rsu.at[s, part], up_sem.at[n])
            chunk[...] += rsu[s, part]

        @pl.when((z <= c) & (z > 0))
        def _():
            arrived(rsd.at[s, part], dn_sem.at[n])
            chunk[...] += rsd[s, part]

        @pl.when((o == 0) & ((t > 0) | (z == c)))
        def _():
            arrived(rsy.at[t, part], ry_sem.at[t, ch])
            chunk[...] += rsy[t, part]

        @pl.when(z > c)
        def _():
            remote(chunk, rsu.at[s, part], s_line.at[n], up_sem.at[n], below).start()

        @pl.when(z < c)
        def _():
            remote(chunk, rsd.at[s, part], s_line.at[n], dn_sem.at[n], above).start()

        @pl.when((z == c) & (o == 1))
        def _():
            remote(chunk, rsy.at[0, part], s_line.at[n], ry_sem.at[0, ch], ypart).start()

        @pl.when((z == c) & (o == 0) & (t > 0))
        def _():
            remote(chunk, y2buf.at[part], s_line.at[n], y2_sem.at[ch], (r, flip(c, t))).start()

        @pl.when((z == c) & (o == 0) & (t == 0))
        def _():
            pltpu.make_async_copy(chunk, y2buf.at[part], y2_sem.at[ch]).start()

    def turn_b(u):
        j, h, t, o = tile_of(u)
        fetch(u).wait()
        fetch(u + 1).start()

        @pl.loop(0, 2)
        def _(i):
            rows = pl.ds(pl.multiple_of(i * piece, piece), piece)
            th, tl = split(tbuf[u % 2, rows])
            q = 2 * h + i
            add = mm(n2h[q], th) + (mm(n2l[q], th) + mm(n2h[q], tl))

            @pl.when((u < 8) & (i == 0))
            def _():
                out2[j] = add

            @pl.when((u >= 8) | (i == 1))
            def _():
                out2[j] += add

    def y_step(q):
        t, ch = pick(Y_T, q // CH), q % CH
        part = pl.ds(pl.multiple_of(ch * wr, wr), wr)
        j = ((y + 1) % 2) * 4 + flip(c, t)
        remote(out2.at[j, part], rsy.at[t, part], s_ry.at[t, ch], ry_sem.at[t, ch], ypart).start()

    def turn_a(u):
        j, h, t, o = tile_of(u)

        @pl.when((h == 0) & (o == 1) & (t >= 1))
        def _():
            for ch in range(CH):
                arrived(n1buf.at[j, pl.ds(ch * cr, cr)], ag_sem.at[j, ch])

        @pl.when(h == 0)
        def _():
            n1h[...], n1l[...] = split(n1buf[j])

        fetch(u).wait()

        @pl.when(u < 31)
        def _():
            fetch(u + 1).start()

        @pl.loop(0, 2)
        def _(i):
            rows = pl.ds(pl.multiple_of(i * piece, piece), piece)
            th, tl = split(tbuf[u % 2, rows])
            add = mm(th, n1h[...]) + (mm(th, n1l[...]) + mm(tl, n1h[...]))
            q = 2 * h + i

            @pl.when(u < 18)
            def _():
                out1[q] = add

            @pl.when(u >= 18)
            def _():
                out1[q] += add

    qx = flip(c, 2)
    end_a = A_TICK[15] + 1
    ag_first = AG_LAG * dist
    ag_rate = jnp.where(z == c, ROOT_RATE, 1)
    rs_first = RS0 + RS_LAG * jnp.where(z > c, 3 - z, jnp.where(z < c, z, jnp.where(c < 2, 3 - c, c)))

    def core_copy(i):
        to = flip(c, 1 + 2 * (1 - i))
        return remote(out1.at[to], cbuf.at[i], s_c.at[i], c_sem.at[i], cpart)

    x_copy = remote(out1.at[qx], xbuf, s_x.at[0], x_sem.at[0], xpart)

    def tick(step, carry):
        @pl.loop(0, ag_rate)
        def _(i):
            n = (step - ag_first) * ag_rate + i

            @pl.when((n >= 0) & (n < 5 * CH))
            def _():
                ag_step(n)

        m = step - rs_first

        @pl.when((m >= 0) & (m < 5 * CH))
        def _():
            rs_step(m)

        @pl.when(step == 8)
        def _():
            got = flip(c, 2)
            arrived(n2buf.at[got], n2_sem.at[2])
            fwd = remote(n2buf.at[got], n2buf.at[got], s_n2.at[2], n2_sem.at[3], cpart)
            fwd.start()
            n2h[got], n2l[got] = split(n2buf[got])
            last = flip(c, 3)
            arrived(n2buf.at[last], n2_sem.at[3])
            n2h[last], n2l[last] = split(n2buf[last])

        @pl.when(step < 16)
        def _():
            turn_b(step)

        for i in range(Y_RATE):
            q = (step - Y0) * Y_RATE + i

            @pl.when((q >= 0) & (q < 3 * CH))
            def _():
                y_step(q)

        @pl.when(sum(jnp.where(step == a, 1, 0) for a in A_TICK) > 0)
        def _():
            turn_a(15 + sum(jnp.where(step >= a, 1, 0) for a in A_TICK))

        @pl.when(step == end_a)
        def _():
            core_copy(0).start()
            core_copy(1).start()

        @pl.when(step == end_a + 1)
        def _():
            core_copy(0).wait_recv()
            out1[qx] += cbuf[0]
            x_copy.start()
            core_copy(1).wait_recv()
            out1[c] += cbuf[1]

        return carry

    last_tick = RS0 + 3 * RS_LAG + 5 * CH
    lax.fori_loop(0, max(last_tick, end_a + 2), tick, 0)

    x_copy.wait_recv()
    y1_out[...] = out1[c] + xbuf[...]
    for ch in range(CH):
        part = pl.ds(ch * wr, wr)
        arrived(y2buf.at[part], y2_sem.at[ch])
    y2_out[...] = y2buf[...]

    def sent(ref, sem):
        pltpu.make_async_copy(ref, ref, sem).wait()

    whole = n2buf.at[0]
    for i in range(3):
        sent(whole, s_n2.at[i])
    for i in range(2):
        sent(cbuf.at[0], s_c.at[i])
    sent(xbuf, s_x.at[0])
    bit = n1buf.at[0, pl.ds(0, cr)]
    wbit = out2.at[0, pl.ds(0, wr)]

    @pl.loop(0, 5 * CH)
    def _(n):
        s, ch = n // CH, n % CH

        @pl.when((z >= c) & (z < 3))
        def _():
            sent(bit, s_up.at[n])

        @pl.when((z <= c) & (z > 0))
        def _():
            sent(bit, s_dn.at[n])

        o, t = pick(AG_O, s), pick(AG_T, s)

        @pl.when((o == 0) & ((t > 0) | (z == c)))
        def _():
            sent(bit, s_y.at[t, ch])

        @pl.when((z != c) | (pick(RS_O, s) == 1) | (pick(RS_T, s) > 0))
        def _():
            sent(wbit, s_line.at[n])

        @pl.when(s < 3)
        def _():
            sent(wbit, s_ry.at[s + 1, ch])

        @pl.when((s == 0) & (c != z))
        def _():
            sent(bit, s_root.at[ch])


def panels(trailing, f1, inv1, f2, inv2, mask1, mask2):
    piece, width = f1.shape
    dma = pltpu.SemaphoreType.DMA
    vm = pltpu.VMEM
    scratch = [
        vm((8, piece, width), F32),
        vm((4, width, piece), F32),
        vm((4, width, piece), BF16),
        vm((4, width, piece), BF16),
        vm((4, piece, width), F32),
        vm((8, width, piece), F32),
        vm((5, width, piece), F32),
        vm((5, width, piece), F32),
        vm((4, width, piece), F32),
        vm((width, piece), F32),
        vm((2, 2 * piece, piece), F32),
        vm((piece, width), BF16),
        vm((piece, width), BF16),
        vm((2, piece, width), F32),
        vm((piece, width), F32),
        dma((4,)), dma((8, CH)), dma((4,)), dma((5 * CH,)), dma((5 * CH,)), dma((4, CH)), dma((CH,)), dma((2,)), dma((2,)), dma((1,)),
        dma((5 * CH,)), dma((5 * CH,)), dma((4, CH)), dma((CH,)), dma((3,)), dma((4, CH)), dma((5 * CH,)), dma((2,)), dma((1,)),
    ]
    anyspace = pl.BlockSpec(memory_space=pl.ANY)
    inv = pl.BlockSpec(memory_space=pltpu.VMEM)
    return pl.pallas_call(
        panels_kernel,
        out_shape=(
            jax.ShapeDtypeStruct((piece, width), F32),
            jax.ShapeDtypeStruct((width, piece), F32),
        )
        * 2,
        in_specs=[anyspace] * 5 + [inv, inv],
        out_specs=(inv,) * 4,
        scratch_shapes=scratch,
        compiler_params=pltpu.CompilerParams(
            collective_id=0, has_side_effects=True, vmem_limit_bytes=63 * 2**20
        ),
        name="panels",
    )(trailing, f1, inv1, f2, inv2, mask1, mask2)


def finish_kernel(
    y1, y2t, n1, n2t, mask1, mask2, inv1, inv2, f_top,
    col1, diag1, col2, cross2, diag2,
    part0, part1, part2, sum0, sum1, sum2, top, top_t, square1, square2,
    acc, got1, got2, got3, got4, recv, send, z_recv, z_send, z_back, z_out,
):
    parts, outs = (part0, part1, part2), (sum0, sum1, sum2)
    r, c = lax.axis_index("row"), lax.axis_index("col")
    z, y, x, k = r // 2, r % 2, c // 2, c % 2
    ypart = (r + 1 - 2 * y, c)
    cpart = (r, flip(c, 1))
    xpart = (r, flip(c, 2))
    rows, cols = parts[0].shape
    h1, h2, h3, h4 = rows // 2, rows // 4, rows // 8, rows // 32
    side = [pl.ds(0, cols // 2), pl.ds(cols // 2, cols // 2)]
    first, second = (x, y), (y, x)
    one, two = (xpart, ypart), (ypart, xpart)
    base = k * h1
    at1 = [first[i] * h2 for i in (0, 1)]
    at2 = [at1[i] + second[i] * h3 for i in (0, 1)]
    line = [(lax.rem(r + 2 * d, 8), c) for d in (1, 2, 3)]

    def remote(src, dst, s_sem, r_sem, to):
        return pltpu.make_async_remote_copy(
            src_ref=src, dst_ref=dst, send_sem=s_sem, recv_sem=r_sem, device_id=to, device_id_type=MESH
        )

    def span(start, size):
        return pl.ds(pl.multiple_of(start, size), size)

    bar = pltpu.get_barrier_semaphore()
    for to in [ypart, cpart, xpart] + line:
        pl.semaphore_signal(bar, inc=1, device_id=to, device_id_type=MESH)
    pl.semaphore_wait(bar, 6)

    def copies(m, stage):
        if stage == 0:
            return [remote(parts[m].at[span((1 - k) * h1, h1)], got1.at[m], send.at[m, 0, 0], recv.at[m, 0, 0], cpart)]
        if stage == 1:
            return [
                remote(acc.at[m, span((1 - first[i]) * h2, h2), side[i]], got2.at[m, i], send.at[m, 1, i], recv.at[m, 1, i], one[i])
                for i in (0, 1)
            ]
        if stage == 2:
            return [
                remote(
                    acc.at[m, span(at1[i] + (1 - second[i]) * h3, h3), side[i]],
                    got3.at[m, i], send.at[m, 2, i], recv.at[m, 2, i], two[i],
                )
                for i in (0, 1)
            ]
        if stage == 3:
            return [
                remote(
                    acc.at[m, span(at2[i] + lax.rem(z + d, 4) * h4, h4), side[i]],
                    got4.at[m, d - 1, i], z_send.at[m, d - 1, i], z_recv.at[m, d - 1, i], line[d - 1],
                )
                for d in (1, 2, 3)
                for i in (0, 1)
            ]
        if stage == 4:
            places = [outs[m].at[span(base + at2[i] + z * h4, h4), side[i]] for i in (0, 1)]
            return [
                remote(places[i], places[i], z_out.at[m, d - 1, i], z_back.at[m, d - 1, i], line[d - 1])
                for d in (1, 2, 3)
                for i in (0, 1)
            ]
        if stage == 7:
            place = outs[m].at[span(base, h1)]
            return [remote(place, place, send.at[m, 5, 0], recv.at[m, 5, 0], cpart)]
        to = (two, one)[stage - 5]
        size, at = ((h3, at2), (h2, at1))[stage - 5]
        places = [outs[m].at[span(base + at[i], size), side[i]] for i in (0, 1)]
        return [remote(places[i], places[i], send.at[m, stage - 2, i], recv.at[m, stage - 2, i], to[i]) for i in (0, 1)]

    def take(m, stage):
        for cp in copies(m, stage):
            cp.wait_recv()
        if stage == 0:
            acc[m] = parts[m][span(base, h1)] + got1[m]
        for i in (0, 1):
            if stage == 1:
                acc[m, span(at1[i], h2), side[i]] += got2[m, i]
            if stage == 2:
                acc[m, span(at2[i], h3), side[i]] += got3[m, i]
            if stage == 3:
                mine = acc[m, span(at2[i] + z * h4, h4), side[i]] + got4[m, 0, i] + (got4[m, 1, i] + got4[m, 2, i])
                outs[m][span(base + at2[i] + z * h4, h4), side[i]] = mine

    def make(m):
        if m == 0:
            col1[...] = -mask1[...] * y1[...]
            part0[...] = mm3(n1[...].T, col1[...])
        if m == 1:
            part1[...] = mm3(n2t[...], col1[...])
            top[...] = mm3(f_top[...], inv2[...])
        if m == 2:
            col2[...] = -mask2[...] * (y2t[...].T + mm3(col1[...], top[...]))
            part2[...] = mm3(n2t[...], col2[...])

    for step in range(8 + 3):
        if step == 3:
            square1[...] = mm3(inv1[...].T, inv1[...])
        if step == 4:
            square2[...] = mm3(inv2[...].T, inv2[...])
        if step == 5:
            top_t[...] = top[...].T
        for m in range(3):
            stage = step - m
            if stage == 0:
                make(m)
            if 1 <= stage <= 8:
                take(m, stage - 1)
            if 0 <= stage < 8:
                for cp in copies(m, stage):
                    cp.start()
        if step == 9:
            diag1[...] = square1[...] - sum0[...]
            cross2[...] = -(mm3(diag1[...], top[...]) + sum1[...].T)
            square2[...] -= mm3(top_t[...], cross2[...])
    diag2[...] = square2[...] - sum2[...]
    for m in range(3):
        for stage in range(8):
            for cp in copies(m, stage):
                cp.wait_send()


def finish(y1, y2t, n1, n2t, mask1, mask2, inv1, inv2, f_top):
    rows, cols = y1.shape
    w = cols // 2
    dma = pltpu.SemaphoreType.DMA
    vm = pltpu.VMEM
    inv = pl.BlockSpec(memory_space=pltpu.VMEM)
    return pl.pallas_call(
        finish_kernel,
        out_shape=(jax.ShapeDtypeStruct((rows, cols), F32),) * 5,
        in_specs=[inv] * 9,
        out_specs=(inv,) * 5,
        scratch_shapes=[
            *[vm((rows, cols), F32)] * 10,
            vm((3, rows // 2, cols), F32),
            vm((3, rows // 2, cols), F32),
            vm((3, 2, rows // 4, w), F32),
            vm((3, 2, rows // 8, w), F32),
            vm((3, 3, 2, rows // 32, w), F32),
            dma((3, 6, 2)), dma((3, 6, 2)),
            dma((3, 3, 2)), dma((3, 3, 2)), dma((3, 3, 2)), dma((3, 3, 2)),
        ],
        compiler_params=pltpu.CompilerParams(
            collective_id=1, has_side_effects=True, vmem_limit_bytes=60 * 2**20
        ),
        name="finish",
    )(y1, y2t, n1, n2t, mask1, mask2, inv1, inv2, f_top)


def column_panel(normal):
    rows, cols = lax.axis_size("row"), lax.axis_size("col")
    moves = [(p, (p % rows) * cols + p // rows) for p in range(rows * cols)]
    piece = lax.ppermute(normal, ("row", "col"), moves)
    return lax.all_gather(piece, "row", axis=0, tiled=True)


def sweep(trailing, col_block):
    part = big_product(trailing, col_block)
    return lax.psum_scatter(part, "col", scatter_dimension=0, tiled=True)


def body(
    special,
    trailing,
    factor_one,
    inverse_one,
    factor_two_top,
    factor_two,
    inverse_two,
    structure_one,
    structure_two,
):
    piece_rows = factor_one.shape[0]
    row_index = lax.axis_index("row")
    col_index = lax.axis_index("col")
    first_row = (row_index * lax.axis_size("col") + col_index) * piece_rows
    mask_one = block_flags(structure_one, first_row, piece_rows)
    mask_two = block_flags(structure_two, first_row, piece_rows)
    if special and piece_rows == factor_one.shape[1]:
        sums = panels(trailing, factor_one, inverse_one, factor_two, inverse_two, mask_one, mask_two)
        return finish(*sums, mask_one, mask_two, inverse_one, inverse_two, factor_two_top)
    normal_one = mask_one * product(factor_one, inverse_one)
    normal_two = mask_two * product(factor_two, inverse_two)
    normal_top = product(factor_two_top, inverse_two)
    column_one = -mask_one * sweep(trailing, column_panel(normal_one))
    column_two = -mask_two * (sweep(trailing, column_panel(normal_two)) + product(column_one, normal_top))
    parts = (
        product(normal_one.T, column_one),
        product(column_one.T, normal_two),
        product(normal_two.T, column_two),
    )
    first, cross, second = lax.psum(parts, ("row", "col"))
    diagonal_one = product(inverse_one.T, inverse_one) - first
    cross_two = -(product(diagonal_one, normal_top) + cross)
    diagonal_two = product(inverse_two.T, inverse_two) - product(normal_top.T, cross_two) - second
    return (column_one, diagonal_one, column_two, cross_two, diagonal_two)


def solution(mesh):
    special = mesh.shape["row"] == 8 and mesh.shape["col"] == 4
    return jax.shard_map(
        functools.partial(body, special),
        mesh=mesh,
        in_specs=(
            P("row", "col"),
            P(("row", "col"), None),
            P(),
            P(),
            P(("row", "col"), None),
            P(),
            P(),
            P(),
        ),
        out_specs=(P(("row", "col"), None), P(), P(("row", "col"), None), P(), P()),
        check_vma=False,
    )
```

```python
import functools

import jax
import jax.numpy as jnp
from jax import lax
from jax.experimental import pallas as pl
from jax.experimental.pallas import tpu as pltpu
from jax.sharding import PartitionSpec as P

BLK = 128
MESH = pl.DeviceIdType.MESH
CH = 8
AG_LAG = 1
RS_LAG = 4
RS0 = 10
Y0 = 9
Y_RATE = 2
ROOT_RATE = 2
AG_O, AG_T = (0, 0, 0, 0, 1), (1, 0, 2, 3, 0)
RS_O, RS_T = (1, 0, 0, 0, 0), (0, 3, 2, 1, 0)
B_O, B_T = (1, 1, 0, 1, 0, 1, 0, 0), (0, 3, 3, 2, 2, 1, 1, 0)
A_O, A_T = (0, 0, 1, 0, 0, 1, 1, 1), (1, 0, 1, 2, 3, 2, 0, 3)
Y_T = (3, 2, 1)
A_TICK = (16, 17, 19, 20, 21, 22, 27, 28, 35, 36, 37, 38, 43, 44, 45, 46)
F32 = jnp.float32
BF16 = jnp.bfloat16


def product(left, right):
    return jnp.dot(left, right, precision=lax.Precision.HIGHEST, preferred_element_type=jnp.float32)


def big_product(left, right):
    return jnp.dot(left, right, precision=lax.Precision.HIGH, preferred_element_type=jnp.float32)


def block_flags(structure, first_row, count):
    blocks = (first_row + jnp.arange(count, dtype=jnp.int32)) // BLK
    hits = jnp.any(blocks[:, None] == structure[None, :], axis=1)
    return hits.astype(jnp.float32)[:, None]


def split(value):
    high = value.astype(BF16)
    return high, (value - high.astype(F32)).astype(BF16)


def mm(left, right):
    return jnp.dot(left, right, preferred_element_type=F32)


def mm3(left, right):
    lh, ll = split(left)
    rh, rl = split(right)
    return mm(lh, rh) + (mm(ll, rh) + mm(lh, rl))


def flip(c, t):
    return ((c // 2 + t // 2) % 2) * 2 + (c % 2 + t % 2) % 2


def pick(table, index):
    return sum(jnp.where(index == i, v, 0) for i, v in enumerate(table) if v)


def row_mask(blocks, piece):
    first = (lax.axis_index("row") * lax.axis_size("col") + lax.axis_index("col")) * piece
    listed = blocks[...]
    rows = first + lax.broadcasted_iota(jnp.int32, (piece, listed.shape[1]), 0)
    hits = jnp.where(rows // BLK == listed, 1.0, 0.0)
    return jnp.max(hits, axis=1, keepdims=True)


def panels_kernel(
    trail, f1, inv1, f2, inv2, list1, list2, y1_out, y2_out, n1_in, n2_in,
    n1buf, n2buf, n2h, n2l, out1, out2, rsu, rsd, rsy, y2buf, tbuf, n1h, n1l, cbuf, xbuf,
    f_sem, ag_sem, n2_sem, up_sem, dn_sem, ry_sem, y2_sem, t_sem, c_sem, x_sem,
    s_up, s_dn, s_y, s_root, s_n2, s_ry, s_line, s_c, s_x,
):
    r, c = lax.axis_index("row"), lax.axis_index("col")
    z, y, x, k = r // 2, r % 2, c // 2, c % 2
    piece = n1_in.shape[0]
    cr = piece // CH
    wr = n2_in.shape[0] // CH
    ypart = (r + 1 - 2 * y, c)
    cpart = (r, flip(c, 1))
    xpart = (r, flip(c, 2))
    above = (lax.rem(r + 2, 8), c)
    below = (lax.rem(r + 6, 8), c)
    dist = jnp.where(z > c, z - c, c - z)

    def remote(src, dst, send, recv, to):
        return pltpu.make_async_remote_copy(
            src_ref=src, dst_ref=dst, send_sem=send, recv_sem=recv, device_id=to, device_id_type=MESH
        )

    def arrived(ref, sem):
        pltpu.make_async_copy(ref, ref, sem).wait()

    bar = pltpu.get_barrier_semaphore()
    for to in (ypart, cpart, xpart, (r, flip(c, 3))):
        pl.semaphore_signal(bar, inc=1, device_id=to, device_id_type=MESH)

    @pl.when(z < 3)
    def _():
        pl.semaphore_signal(bar, inc=1, device_id=above, device_id_type=MESH)

    @pl.when(z > 0)
    def _():
        pl.semaphore_signal(bar, inc=1, device_id=below, device_id_type=MESH)

    def tile_of(u):
        isa = u // 16
        v = u % 16
        hb, ha = (x + v // 8) % 2, v % 2
        pb, pa = v % 8, v // 2
        t = isa * pick(A_T, pa) + (1 - isa) * pick(B_T, pb)
        o = isa * pick(A_O, pa) + (1 - isa) * pick(B_O, pb)
        h = isa * ha + (1 - isa) * hb
        return ((y + o) % 2) * 4 + flip(c, t), h, t, o

    half = 2 * piece

    def fetch(u):
        j, h, _, _ = tile_of(u)
        rows = pl.ds(pl.multiple_of(h * half, half), half)
        cols = pl.ds(pl.multiple_of(j * piece, piece), piece)
        return pltpu.make_async_copy(trail.at[rows, cols], tbuf.at[u % 2], t_sem.at[u % 2])

    fetch(0).start()
    loads = [pltpu.make_async_copy(a, out2.at[i], f_sem.at[i]) for i, a in enumerate((f2, inv2, f1, inv1))]
    for cp in loads:
        cp.start()
    loads[0].wait()
    loads[1].wait()
    n2_in[...] = (row_mask(list2, piece) * mm3(out2[0], out2[1])).T
    own = pltpu.make_async_copy(n2_in, n2buf.at[c], n2_sem.at[0])
    own.start()

    pl.semaphore_wait(bar, 4 + (z + 2) // 3 + (5 - z) // 3)

    to_x = remote(n2_in, n2buf.at[c], s_n2.at[0], n2_sem.at[2], xpart)
    to_x.start()
    to_c = remote(n2_in, n2buf.at[c], s_n2.at[1], n2_sem.at[1], cpart)
    to_c.start()

    loads[2].wait()
    loads[3].wait()
    n1_in[...] = row_mask(list1, piece) * mm3(out2[2], out2[3])
    here = y * 4 + c
    for ch in range(CH):
        part = pl.ds(ch * cr, cr)

        @pl.when(c == z)
        def _():
            pltpu.make_async_copy(n1_in.at[part], n1buf.at[here, part], ag_sem.at[here, ch]).start()

        @pl.when(c != z)
        def _():
            remote(n1_in.at[part], n1buf.at[here, part], s_root.at[ch], ag_sem.at[here, ch], (r, z)).start()

    own.wait()
    arrived(n2buf.at[flip(c, 1)], n2_sem.at[1])
    for t in range(2):
        q = flip(c, t)
        n2h[q], n2l[q] = split(n2buf[q])

    def ag_step(n):
        s, ch = n // CH, n % CH
        o, t = pick(AG_O, s), pick(AG_T, s)
        j = ((y + o) % 2) * 4 + flip(c, t)
        part = pl.ds(pl.multiple_of(ch * cr, cr), cr)
        chunk = n1buf.at[j, part]
        arrived(chunk, ag_sem.at[j, ch])

        @pl.when((z >= c) & (z < 3))
        def _():
            remote(chunk, chunk, s_up.at[n], ag_sem.at[j, ch], above).start()

        @pl.when((z <= c) & (z > 0))
        def _():
            remote(chunk, chunk, s_dn.at[n], ag_sem.at[j, ch], below).start()

        @pl.when((o == 0) & ((t > 0) | (z == c)))
        def _():
            remote(chunk, chunk, s_y.at[t, ch], ag_sem.at[j, ch], ypart).start()

    def rs_step(n):
        s, ch = n // CH, n % CH
        o, t = pick(RS_O, s), pick(RS_T, s)
        j = ((y + o) % 2) * 4 + flip(c, t)
        part = pl.ds(pl.multiple_of(ch * wr, wr), wr)
        chunk = out2.at[j, part]

        @pl.when((z >= c) & (z < 3))
        def _():
            arrived(rsu.at[s, part], up_sem.at[n])
            chunk[...] += rsu[s, part]

        @pl.when((z <= c) & (z > 0))
        def _():
            arrived(rsd.at[s, part], dn_sem.at[n])
            chunk[...] += rsd[s, part]

        @pl.when((o == 0) & ((t > 0) | (z == c)))
        def _():
            arrived(rsy.at[t, part], ry_sem.at[t, ch])
            chunk[...] += rsy[t, part]

        @pl.when(z > c)
        def _():
            remote(chunk, rsu.at[s, part], s_line.at[n], up_sem.at[n], below).start()

        @pl.when(z < c)
        def _():
            remote(chunk, rsd.at[s, part], s_line.at[n], dn_sem.at[n], above).start()

        @pl.when((z == c) & (o == 1))
        def _():
            remote(chunk, rsy.at[0, part], s_line.at[n], ry_sem.at[0, ch], ypart).start()

        @pl.when((z == c) & (o == 0) & (t > 0))
        def _():
            remote(chunk, y2buf.at[part], s_line.at[n], y2_sem.at[ch], (r, flip(c, t))).start()

        @pl.when((z == c) & (o == 0) & (t == 0))
        def _():
            pltpu.make_async_copy(chunk, y2buf.at[part], y2_sem.at[ch]).start()

    def turn_b(u):
        j, h, t, o = tile_of(u)
        fetch(u).wait()
        fetch(u + 1).start()

        @pl.loop(0, 2)
        def _(i):
            rows = pl.ds(pl.multiple_of(i * piece, piece), piece)
            th, tl = split(tbuf[u % 2, rows])
            q = 2 * h + i
            add = mm(n2h[q], th) + (mm(n2l[q], th) + mm(n2h[q], tl))

            @pl.when((u < 8) & (i == 0))
            def _():
                out2[j] = add

            @pl.when((u >= 8) | (i == 1))
            def _():
                out2[j] += add

    def y_step(q):
        t, ch = pick(Y_T, q // CH), q % CH
        part = pl.ds(pl.multiple_of(ch * wr, wr), wr)
        j = ((y + 1) % 2) * 4 + flip(c, t)
        remote(out2.at[j, part], rsy.at[t, part], s_ry.at[t, ch], ry_sem.at[t, ch], ypart).start()

    def turn_a(u):
        j, h, t, o = tile_of(u)

        @pl.when((h == 0) & (o == 1) & (t >= 1))
        def _():
            for ch in range(CH):
                arrived(n1buf.at[j, pl.ds(ch * cr, cr)], ag_sem.at[j, ch])

        @pl.when(h == 0)
        def _():
            n1h[...], n1l[...] = split(n1buf[j])

        fetch(u).wait()

        @pl.when(u < 31)
        def _():
            fetch(u + 1).start()

        @pl.loop(0, 2)
        def _(i):
            rows = pl.ds(pl.multiple_of(i * piece, piece), piece)
            th, tl = split(tbuf[u % 2, rows])
            add = mm(th, n1h[...]) + (mm(th, n1l[...]) + mm(tl, n1h[...]))
            q = 2 * h + i

            @pl.when(u < 18)
            def _():
                out1[q] = add

            @pl.when(u >= 18)
            def _():
                out1[q] += add

    qx = flip(c, 2)
    end_a = A_TICK[15] + 1
    ag_first = AG_LAG * dist
    ag_rate = jnp.where(z == c, ROOT_RATE, 1)
    rs_first = RS0 + RS_LAG * jnp.where(z > c, 3 - z, jnp.where(z < c, z, jnp.where(c < 2, 3 - c, c)))

    def core_copy(i):
        to = flip(c, 1 + 2 * (1 - i))
        return remote(out1.at[to], cbuf.at[i], s_c.at[i], c_sem.at[i], cpart)

    x_copy = remote(out1.at[qx], xbuf, s_x.at[0], x_sem.at[0], xpart)

    def tick(step, carry):
        @pl.loop(0, ag_rate)
        def _(i):
            n = (step - ag_first) * ag_rate + i

            @pl.when((n >= 0) & (n < 5 * CH))
            def _():
                ag_step(n)

        m = step - rs_first

        @pl.when((m >= 0) & (m < 5 * CH))
        def _():
            rs_step(m)

        @pl.when(step == 8)
        def _():
            got = flip(c, 2)
            arrived(n2buf.at[got], n2_sem.at[2])
            fwd = remote(n2buf.at[got], n2buf.at[got], s_n2.at[2], n2_sem.at[3], cpart)
            fwd.start()
            n2h[got], n2l[got] = split(n2buf[got])
            last = flip(c, 3)
            arrived(n2buf.at[last], n2_sem.at[3])
            n2h[last], n2l[last] = split(n2buf[last])

        @pl.when(step < 16)
        def _():
            turn_b(step)

        for i in range(Y_RATE):
            q = (step - Y0) * Y_RATE + i

            @pl.when((q >= 0) & (q < 3 * CH))
            def _():
                y_step(q)

        @pl.when(sum(jnp.where(step == a, 1, 0) for a in A_TICK) > 0)
        def _():
            turn_a(15 + sum(jnp.where(step >= a, 1, 0) for a in A_TICK))

        @pl.when(step == end_a)
        def _():
            core_copy(0).start()
            core_copy(1).start()

        @pl.when(step == end_a + 1)
        def _():
            core_copy(0).wait_recv()
            out1[qx] += cbuf[0]
            x_copy.start()
            core_copy(1).wait_recv()
            out1[c] += cbuf[1]

        return carry

    last_tick = RS0 + 3 * RS_LAG + 5 * CH
    lax.fori_loop(0, max(last_tick, end_a + 2), tick, 0)

    x_copy.wait_recv()
    y1_out[...] = out1[c] + xbuf[...]
    for ch in range(CH):
        part = pl.ds(ch * wr, wr)
        arrived(y2buf.at[part], y2_sem.at[ch])
    y2_out[...] = y2buf[...]

    def sent(ref, sem):
        pltpu.make_async_copy(ref, ref, sem).wait()

    whole = n2buf.at[0]
    for i in range(3):
        sent(whole, s_n2.at[i])
    for i in range(2):
        sent(cbuf.at[0], s_c.at[i])
    sent(xbuf, s_x.at[0])
    bit = n1buf.at[0, pl.ds(0, cr)]
    wbit = out2.at[0, pl.ds(0, wr)]

    @pl.loop(0, 5 * CH)
    def _(n):
        s, ch = n // CH, n % CH

        @pl.when((z >= c) & (z < 3))
        def _():
            sent(bit, s_up.at[n])

        @pl.when((z <= c) & (z > 0))
        def _():
            sent(bit, s_dn.at[n])

        o, t = pick(AG_O, s), pick(AG_T, s)

        @pl.when((o == 0) & ((t > 0) | (z == c)))
        def _():
            sent(bit, s_y.at[t, ch])

        @pl.when((z != c) | (pick(RS_O, s) == 1) | (pick(RS_T, s) > 0))
        def _():
            sent(wbit, s_line.at[n])

        @pl.when(s < 3)
        def _():
            sent(wbit, s_ry.at[s + 1, ch])

        @pl.when((s == 0) & (c != z))
        def _():
            sent(bit, s_root.at[ch])


def panels(trailing, f1, inv1, f2, inv2, list1, list2):
    piece, width = f1.shape
    dma = pltpu.SemaphoreType.DMA
    vm = pltpu.VMEM
    scratch = [
        vm((8, piece, width), F32),
        vm((4, width, piece), F32),
        vm((4, width, piece), BF16),
        vm((4, width, piece), BF16),
        vm((4, piece, width), F32),
        vm((8, width, piece), F32),
        vm((5, width, piece), F32),
        vm((5, width, piece), F32),
        vm((4, width, piece), F32),
        vm((width, piece), F32),
        vm((2, 2 * piece, piece), F32),
        vm((piece, width), BF16),
        vm((piece, width), BF16),
        vm((2, piece, width), F32),
        vm((piece, width), F32),
        dma((4,)), dma((8, CH)), dma((4,)), dma((5 * CH,)), dma((5 * CH,)), dma((4, CH)), dma((CH,)), dma((2,)), dma((2,)), dma((1,)),
        dma((5 * CH,)), dma((5 * CH,)), dma((4, CH)), dma((CH,)), dma((3,)), dma((4, CH)), dma((5 * CH,)), dma((2,)), dma((1,)),
    ]
    anyspace = pl.BlockSpec(memory_space=pl.ANY)
    inv = pl.BlockSpec(memory_space=pltpu.VMEM)
    return pl.pallas_call(
        panels_kernel,
        out_shape=(
            jax.ShapeDtypeStruct((piece, width), F32),
            jax.ShapeDtypeStruct((width, piece), F32),
        )
        * 2,
        in_specs=[anyspace] * 5 + [inv, inv],
        out_specs=(inv,) * 4,
        scratch_shapes=scratch,
        compiler_params=pltpu.CompilerParams(
            collective_id=0, has_side_effects=True, vmem_limit_bytes=63 * 2**20
        ),
        name="panels",
    )(trailing, f1, inv1, f2, inv2, list1, list2)


def finish_kernel(
    y1, y2t, n1, n2t, list1, list2, inv1, inv2, f_top,
    col1, diag1, col2, cross2, diag2,
    part0, part1, part2, sum0, sum1, sum2, top, top_t, square1, square2,
    acc, got1, got2, got3, got4, recv, send, z_recv, z_send, z_back, z_out,
):
    parts, outs = (part0, part1, part2), (sum0, sum1, sum2)
    r, c = lax.axis_index("row"), lax.axis_index("col")
    z, y, x, k = r // 2, r % 2, c // 2, c % 2
    ypart = (r + 1 - 2 * y, c)
    cpart = (r, flip(c, 1))
    xpart = (r, flip(c, 2))
    rows, cols = parts[0].shape
    h1, h2, h3, h4 = rows // 2, rows // 4, rows // 8, rows // 32
    side = [pl.ds(0, cols // 2), pl.ds(cols // 2, cols // 2)]
    first, second = (x, y), (y, x)
    one, two = (xpart, ypart), (ypart, xpart)
    base = k * h1
    at1 = [first[i] * h2 for i in (0, 1)]
    at2 = [at1[i] + second[i] * h3 for i in (0, 1)]
    line = [(lax.rem(r + 2 * d, 8), c) for d in (1, 2, 3)]

    def remote(src, dst, s_sem, r_sem, to):
        return pltpu.make_async_remote_copy(
            src_ref=src, dst_ref=dst, send_sem=s_sem, recv_sem=r_sem, device_id=to, device_id_type=MESH
        )

    def span(start, size):
        return pl.ds(pl.multiple_of(start, size), size)

    bar = pltpu.get_barrier_semaphore()
    for to in [ypart, cpart, xpart] + line:
        pl.semaphore_signal(bar, inc=1, device_id=to, device_id_type=MESH)
    pl.semaphore_wait(bar, 6)

    def copies(m, stage):
        if stage == 0:
            return [remote(parts[m].at[span((1 - k) * h1, h1)], got1.at[m], send.at[m, 0, 0], recv.at[m, 0, 0], cpart)]
        if stage == 1:
            return [
                remote(acc.at[m, span((1 - first[i]) * h2, h2), side[i]], got2.at[m, i], send.at[m, 1, i], recv.at[m, 1, i], one[i])
                for i in (0, 1)
            ]
        if stage == 2:
            return [
                remote(
                    acc.at[m, span(at1[i] + (1 - second[i]) * h3, h3), side[i]],
                    got3.at[m, i], send.at[m, 2, i], recv.at[m, 2, i], two[i],
                )
                for i in (0, 1)
            ]
        if stage == 3:
            return [
                remote(
                    acc.at[m, span(at2[i] + lax.rem(z + d, 4) * h4, h4), side[i]],
                    got4.at[m, d - 1, i], z_send.at[m, d - 1, i], z_recv.at[m, d - 1, i], line[d - 1],
                )
                for d in (1, 2, 3)
                for i in (0, 1)
            ]
        if stage == 4:
            places = [outs[m].at[span(base + at2[i] + z * h4, h4), side[i]] for i in (0, 1)]
            return [
                remote(places[i], places[i], z_out.at[m, d - 1, i], z_back.at[m, d - 1, i], line[d - 1])
                for d in (1, 2, 3)
                for i in (0, 1)
            ]
        if stage == 7:
            place = outs[m].at[span(base, h1)]
            return [remote(place, place, send.at[m, 5, 0], recv.at[m, 5, 0], cpart)]
        to = (two, one)[stage - 5]
        size, at = ((h3, at2), (h2, at1))[stage - 5]
        places = [outs[m].at[span(base + at[i], size), side[i]] for i in (0, 1)]
        return [remote(places[i], places[i], send.at[m, stage - 2, i], recv.at[m, stage - 2, i], to[i]) for i in (0, 1)]

    def take(m, stage):
        for cp in copies(m, stage):
            cp.wait_recv()
        if stage == 0:
            acc[m] = parts[m][span(base, h1)] + got1[m]
        for i in (0, 1):
            if stage == 1:
                acc[m, span(at1[i], h2), side[i]] += got2[m, i]
            if stage == 2:
                acc[m, span(at2[i], h3), side[i]] += got3[m, i]
            if stage == 3:
                mine = acc[m, span(at2[i] + z * h4, h4), side[i]] + got4[m, 0, i] + (got4[m, 1, i] + got4[m, 2, i])
                outs[m][span(base + at2[i] + z * h4, h4), side[i]] = mine

    def make(m):
        if m == 0:
            col1[...] = -row_mask(list1, rows) * y1[...]
            part0[...] = mm3(n1[...].T, col1[...])
        if m == 1:
            part1[...] = mm3(n2t[...], col1[...])
            top[...] = mm3(f_top[...], inv2[...])
        if m == 2:
            col2[...] = -row_mask(list2, rows) * (y2t[...].T + mm3(col1[...], top[...]))
            part2[...] = mm3(n2t[...], col2[...])

    for step in range(8 + 3):
        if step == 3:
            square1[...] = mm3(inv1[...].T, inv1[...])
        if step == 4:
            square2[...] = mm3(inv2[...].T, inv2[...])
        if step == 5:
            top_t[...] = top[...].T
        for m in range(3):
            stage = step - m
            if stage == 0:
                make(m)
            if 1 <= stage <= 8:
                take(m, stage - 1)
            if 0 <= stage < 8:
                for cp in copies(m, stage):
                    cp.start()
        if step == 9:
            diag1[...] = square1[...] - sum0[...]
            cross2[...] = -(mm3(diag1[...], top[...]) + sum1[...].T)
            square2[...] -= mm3(top_t[...], cross2[...])
    diag2[...] = square2[...] - sum2[...]
    for m in range(3):
        for stage in range(8):
            for cp in copies(m, stage):
                cp.wait_send()


def finish(y1, y2t, n1, n2t, list1, list2, inv1, inv2, f_top):
    rows, cols = y1.shape
    w = cols // 2
    dma = pltpu.SemaphoreType.DMA
    vm = pltpu.VMEM
    inv = pl.BlockSpec(memory_space=pltpu.VMEM)
    return pl.pallas_call(
        finish_kernel,
        out_shape=(jax.ShapeDtypeStruct((rows, cols), F32),) * 5,
        in_specs=[inv] * 9,
        out_specs=(inv,) * 5,
        scratch_shapes=[
            *[vm((rows, cols), F32)] * 10,
            vm((3, rows // 2, cols), F32),
            vm((3, rows // 2, cols), F32),
            vm((3, 2, rows // 4, w), F32),
            vm((3, 2, rows // 8, w), F32),
            vm((3, 3, 2, rows // 32, w), F32),
            dma((3, 6, 2)), dma((3, 6, 2)),
            dma((3, 3, 2)), dma((3, 3, 2)), dma((3, 3, 2)), dma((3, 3, 2)),
        ],
        compiler_params=pltpu.CompilerParams(
            collective_id=1, has_side_effects=True, vmem_limit_bytes=60 * 2**20
        ),
        name="finish",
    )(y1, y2t, n1, n2t, list1, list2, inv1, inv2, f_top)


def hand_over_kernel(*refs):
    for i in range(5):
        refs[5 + i][...] = refs[i][...]


def hand_over(arrays):
    inv = pl.BlockSpec(memory_space=pltpu.VMEM)
    return pl.pallas_call(
        hand_over_kernel,
        out_shape=tuple(jax.ShapeDtypeStruct(a.shape, a.dtype) for a in arrays),
        in_specs=[inv] * 5,
        out_specs=(inv,) * 5,
        name="hand_over",
    )(*arrays)


def column_panel(normal):
    rows, cols = lax.axis_size("row"), lax.axis_size("col")
    moves = [(p, (p % rows) * cols + p // rows) for p in range(rows * cols)]
    piece = lax.ppermute(normal, ("row", "col"), moves)
    return lax.all_gather(piece, "row", axis=0, tiled=True)


def sweep(trailing, col_block):
    part = big_product(trailing, col_block)
    return lax.psum_scatter(part, "col", scatter_dimension=0, tiled=True)


def body(
    special,
    trailing,
    factor_one,
    inverse_one,
    factor_two_top,
    factor_two,
    inverse_two,
    structure_one,
    structure_two,
):
    piece_rows = factor_one.shape[0]
    if special and piece_rows == factor_one.shape[1]:
        lists = (structure_one[None, :], structure_two[None, :])
        sums = panels(trailing, factor_one, inverse_one, factor_two, inverse_two, *lists)
        return hand_over(finish(*sums, *lists, inverse_one, inverse_two, factor_two_top))
    row_index = lax.axis_index("row")
    col_index = lax.axis_index("col")
    first_row = (row_index * lax.axis_size("col") + col_index) * piece_rows
    mask_one = block_flags(structure_one, first_row, piece_rows)
    mask_two = block_flags(structure_two, first_row, piece_rows)
    normal_one = mask_one * product(factor_one, inverse_one)
    normal_two = mask_two * product(factor_two, inverse_two)
    normal_top = product(factor_two_top, inverse_two)
    column_one = -mask_one * sweep(trailing, column_panel(normal_one))
    column_two = -mask_two * (sweep(trailing, column_panel(normal_two)) + product(column_one, normal_top))
    parts = (
        product(normal_one.T, column_one),
        product(column_one.T, normal_two),
        product(normal_two.T, column_two),
    )
    first, cross, second = lax.psum(parts, ("row", "col"))
    diagonal_one = product(inverse_one.T, inverse_one) - first
    cross_two = -(product(diagonal_one, normal_top) + cross)
    diagonal_two = product(inverse_two.T, inverse_two) - product(normal_top.T, cross_two) - second
    return (column_one, diagonal_one, column_two, cross_two, diagonal_two)


def solution(mesh):
    special = mesh.shape["row"] == 8 and mesh.shape["col"] == 4
    return jax.shard_map(
        functools.partial(body, special),
        mesh=mesh,
        in_specs=(
            P("row", "col"),
            P(("row", "col"), None),
            P(),
            P(),
            P(("row", "col"), None),
            P(),
            P(),
            P(),
        ),
        out_specs=(P(("row", "col"), None), P(), P(("row", "col"), None), P(), P()),
        check_vma=False,
    )
```

```python
import functools

import jax
import jax.numpy as jnp
from jax import lax
from jax.experimental import pallas as pl
from jax.experimental.pallas import tpu as pltpu
from jax.sharding import PartitionSpec as P

BLK = 128
MESH = pl.DeviceIdType.MESH
CH = 8
AG_LAG = 1
RS_LAG = 5
RS0 = 10
Y0 = 16
NEAR0 = 16
ROOT0 = 41
X_TICK = 8
AG_O, AG_T = (0, 0, 0, 0, 1, 1), (1, 0, 2, 3, 0, 1)
RS_O, RS_T = (1, 0, 0, 0, 0), (0, 3, 2, 0, 1)
B_O, B_T = (1, 1, 1, 0, 1, 0, 0, 0), (0, 1, 3, 3, 2, 2, 1, 0)
A_O, A_T = (0, 0, 0, 0, 1, 1, 1, 1), (1, 0, 2, 3, 0, 2, 3, 1)
Y_T = (3, 2, 1)
QR = CH // 2
AG_N = 2 * len(AG_T) * QR
A_TICK = (20, 21, 22, 23, 24, 25, 26, 27, 31, 35, 39, 43, 47, 48, 49, 51)
F32 = jnp.float32
BF16 = jnp.bfloat16


def product(left, right):
    return jnp.dot(left, right, precision=lax.Precision.HIGHEST, preferred_element_type=jnp.float32)


def big_product(left, right):
    return jnp.dot(left, right, precision=lax.Precision.HIGH, preferred_element_type=jnp.float32)


def block_flags(structure, first_row, count):
    blocks = (first_row + jnp.arange(count, dtype=jnp.int32)) // BLK
    hits = jnp.any(blocks[:, None] == structure[None, :], axis=1)
    return hits.astype(jnp.float32)[:, None]


def split(value):
    high = value.astype(BF16)
    return high, (value - high.astype(F32)).astype(BF16)


def mm(left, right):
    return jnp.dot(left, right, preferred_element_type=F32)


def mm3(left, right):
    lh, ll = split(left)
    rh, rl = split(right)
    return mm(lh, rh) + (mm(ll, rh) + mm(lh, rl))


def flip(c, t):
    return ((c // 2 + t // 2) % 2) * 2 + (c % 2 + t % 2) % 2


def pick(table, index):
    return sum(jnp.where(index == i, v, 0) for i, v in enumerate(table) if v)


def row_mask(blocks, piece):
    first = (lax.axis_index("row") * lax.axis_size("col") + lax.axis_index("col")) * piece
    listed = blocks[...]
    rows = first + lax.broadcasted_iota(jnp.int32, (piece, listed.shape[1]), 0)
    hits = jnp.where(rows // BLK == listed, 1.0, 0.0)
    return jnp.max(hits, axis=1, keepdims=True)


def panels_kernel(
    trail, f1, inv1, f2, inv2, list1, list2, y1_out, y2_out, n1_in, n2_in,
    n1buf, n2buf, n2h, n2l, out1, out2, rsu, rsd, rsy, rsn, y2buf, tbuf, n1h, n1l, cbuf, xbuf,
    f_sem, near_sem, ag_sem, n2_sem, up_sem, dn_sem, ry_sem, y2_sem, t_sem, c_sem, x_sem,
    s_up, s_dn, s_y, s_root, s_n2, s_ry, s_line, s_c, s_x,
):
    r, c = lax.axis_index("row"), lax.axis_index("col")
    z, y, x, k = r // 2, r % 2, c // 2, c % 2
    piece = n1_in.shape[0]
    width = n1_in.shape[1]
    cr, gw = piece // QR, width // 2
    wr = n2_in.shape[0] // CH
    ypart = (r + 1 - 2 * y, c)
    cpart = (r, flip(c, 1))
    xpart = (r, flip(c, 2))
    above = (lax.rem(r + 2, 8), c)
    below = (lax.rem(r + 6, 8), c)
    near = jnp.where((z // 2 == x) & (z != c), 1, 0)
    dist = jnp.where(z > c, z - c, c - z)

    def remote(src, dst, send, recv, to):
        return pltpu.make_async_remote_copy(
            src_ref=src, dst_ref=dst, send_sem=send, recv_sem=recv, device_id=to, device_id_type=MESH
        )

    def cols_of(g):
        return pl.ds(pl.multiple_of(g * gw, gw), gw)

    def chunk_of(ch):
        return pl.ds(pl.multiple_of((ch % QR) * cr, cr), cr), cols_of(ch // QR)

    def arrived(ref, sem):
        pltpu.make_async_copy(ref, ref, sem).wait()

    bar = pltpu.get_barrier_semaphore()
    for to in (ypart, cpart, xpart, (r, flip(c, 3))):
        pl.semaphore_signal(bar, inc=1, device_id=to, device_id_type=MESH)

    @pl.when(z < 3)
    def _():
        pl.semaphore_signal(bar, inc=1, device_id=above, device_id_type=MESH)

    @pl.when(z > 0)
    def _():
        pl.semaphore_signal(bar, inc=1, device_id=below, device_id_type=MESH)

    def tile_of(u):
        isa = jnp.where(u >= 16, 1, 0)
        w = (u - 16) * isa
        pb, pa = u % 8, (w // 2) % 8
        t = isa * pick(A_T, pa) + (1 - isa) * pick(B_T, pb)
        o = isa * pick(A_O, pa) + (1 - isa) * pick(B_O, pb)
        h = isa * (w % 2) + (1 - isa) * ((x + u // 8) % 2)
        return ((y + o) % 2) * 4 + flip(c, t), h, t, o

    half = 2 * piece

    def fetch(u):
        j, h, _, _ = tile_of(u)
        rows = pl.ds(pl.multiple_of(h * half, half), half)
        cols = pl.ds(pl.multiple_of(j * piece, piece), piece)
        return pltpu.make_async_copy(trail.at[rows, cols], tbuf.at[u % 2], t_sem.at[u % 2])

    fetch(0).start()
    loads = [pltpu.make_async_copy(a, out2.at[i], f_sem.at[i]) for i, a in enumerate((f2, inv2, f1, inv1))]
    for cp in loads:
        cp.start()
    loads[0].wait()
    loads[1].wait()
    n2_in[...] = (row_mask(list2, piece) * mm3(out2[0], out2[1])).T
    own = pltpu.make_async_copy(n2_in, n2buf.at[c], n2_sem.at[0])
    own.start()

    pl.semaphore_wait(bar, 4 + (z + 2) // 3 + (5 - z) // 3)

    to_x = remote(n2_in, n2buf.at[c], s_n2.at[0], n2_sem.at[2], xpart)
    to_x.start()
    to_c = remote(n2_in, n2buf.at[c], s_n2.at[1], n2_sem.at[1], cpart)
    to_c.start()

    loads[2].wait()
    loads[3].wait()
    n1_in[...] = row_mask(list1, piece) * mm3(out2[2], out2[3])
    here = y * 4 + c
    for ch in range(CH):
        part = chunk_of(ch)

        @pl.when(c == z)
        def _():
            pltpu.make_async_copy(n1_in.at[part], n1buf.at[(here, *part)], ag_sem.at[here, ch]).start()

        @pl.when(c != z)
        def _():
            remote(n1_in.at[part], n1buf.at[(here, *part)], s_root.at[ch], ag_sem.at[here, ch], (r, z)).start()

    own.wait()
    arrived(n2buf.at[flip(c, 1)], n2_sem.at[1])
    for t in range(2):
        q = flip(c, t)
        n2h[q], n2l[q] = split(n2buf[q])

    def ag_of(n):
        g, s, i = n // (len(AG_T) * QR), (n // QR) % len(AG_T), n % QR
        return pick(AG_O, s), pick(AG_T, s), g * QR + i

    def goes_y(o, t):
        return (o == 0) & ((t > 1) | (z == c))

    def ag_step(n):
        o, t, ch = ag_of(n)
        j = ((y + o) % 2) * 4 + flip(c, t)
        chunk = n1buf.at[(j, *chunk_of(ch))]
        arrived(chunk, ag_sem.at[j, ch])

        @pl.when((z >= c) & (z < 3))
        def _():
            remote(chunk, chunk, s_up.at[n], ag_sem.at[j, ch], above).start()

        @pl.when((z <= c) & (z > 0))
        def _():
            remote(chunk, chunk, s_dn.at[n], ag_sem.at[j, ch], below).start()

        @pl.when(goes_y(o, t))
        def _():
            remote(chunk, chunk, s_y.at[t, ch], ag_sem.at[j, ch], ypart).start()

    def rs_step(n):
        s, ch = n // CH, n % CH
        o, t = pick(RS_O, s), pick(RS_T, s)
        j = ((y + o) % 2) * 4 + flip(c, t)
        part = pl.ds(pl.multiple_of(ch * wr, wr), wr)
        chunk = out2.at[j, part]

        @pl.when((z >= c) & (z < 3))
        def _():
            arrived(rsu.at[s, part], up_sem.at[n])
            chunk[...] += rsu[s, part]

        @pl.when((z <= c) & (z > 0))
        def _():
            arrived(rsd.at[s, part], dn_sem.at[n])
            chunk[...] += rsd[s, part]

        @pl.when((o == 0) & ((t > 1) | (z == c) | ((t == 1) & (near == 0))))
        def _():
            arrived(rsy.at[t, part], ry_sem.at[t, ch])
            chunk[...] += rsy[t, part]

        @pl.when(z > c)
        def _():
            remote(chunk, rsu.at[s, part], s_line.at[n], up_sem.at[n], below).start()

        @pl.when(z < c)
        def _():
            remote(chunk, rsd.at[s, part], s_line.at[n], dn_sem.at[n], above).start()

        @pl.when((z == c) & (o == 1))
        def _():
            remote(chunk, rsy.at[0, part], s_line.at[n], ry_sem.at[0, ch], ypart).start()

        @pl.when((z == c) & (o == 0) & (t > 0))
        def _():
            remote(chunk, y2buf.at[part], s_line.at[n], y2_sem.at[ch], (r, flip(c, t))).start()

        @pl.when((z == c) & (o == 0) & (t == 0))
        def _():
            pltpu.make_async_copy(chunk, y2buf.at[part], y2_sem.at[ch]).start()

    def turn_b(u):
        j, h, t, o = tile_of(u)
        fetch(u).wait()
        fetch(u + 1).start()

        @pl.loop(0, 2)
        def _(i):
            rows = pl.ds(pl.multiple_of(i * piece, piece), piece)
            th, tl = split(tbuf[u % 2, rows])
            q = 2 * h + i
            add = mm(n2h[q], th) + (mm(n2l[q], th) + mm(n2h[q], tl))

            @pl.when((u < 8) & (i == 0))
            def _():
                out2[j] = add

            @pl.when((u >= 8) | (i == 1))
            def _():
                out2[j] += add

    def y_step(q):
        t, ch = pick(Y_T, q // CH), q % CH
        part = pl.ds(pl.multiple_of(ch * wr, wr), wr)
        j = ((y + 1) % 2) * 4 + flip(c, t)

        @pl.when((t > 1) | ((near == 0) & (z != c)))
        def _():
            remote(out2.at[j, part], rsy.at[t, part], s_ry.at[t, ch], ry_sem.at[t, ch], ypart).start()

    j_near = ((y + 1) % 2) * 4 + flip(c, 1)

    def near_step(ch):
        part = pl.ds(pl.multiple_of(ch * wr, wr), wr)
        remote(out2.at[j_near, part], rsn.at[part], s_ry.at[1, ch], near_sem.at[ch], (lax.rem(r + jnp.where(z < c, 2, 6), 8), c)).start()

    def root_step(ch):
        part = pl.ds(pl.multiple_of(ch * wr, wr), wr)
        arrived(rsn.at[part], near_sem.at[ch])
        out2[j_near, part] += rsn[part]
        remote(out2.at[j_near, part], rsy.at[1, part], s_ry.at[1, ch], ry_sem.at[1, ch], ypart).start()

    def turn_a(turn):
        g = turn // 8
        cols = cols_of(g)
        j, _, t, o = tile_of(16 + 2 * turn)

        @pl.when((o == 1) & (t >= 2))
        def _():
            for i in range(QR):
                ch = g * QR + i
                arrived(n1buf.at[(j, *chunk_of(ch))], ag_sem.at[j, ch])

        n1h[...], n1l[...] = split(n1buf[j, :, cols])

        @pl.loop(0, 2)
        def _(h):
            u = 16 + 2 * turn + h
            fetch(u).wait()

            @pl.when(u < 47)
            def _():
                fetch(u + 1).start()

            @pl.loop(0, 2)
            def _(i):
                rows = pl.ds(pl.multiple_of(i * piece, piece), piece)
                th, tl = split(tbuf[u % 2, rows])
                add = mm(th, n1h[...]) + (mm(th, n1l[...]) + mm(tl, n1h[...]))
                q = 2 * h + i

                @pl.when(turn % 8 == 0)
                def _():
                    out1[q, :, cols] = add

                @pl.when(turn % 8 > 0)
                def _():
                    out1[q, :, cols] += add

    qx = flip(c, 2)
    ag_first = AG_LAG * dist
    rs_first = RS0 + RS_LAG * jnp.where(z > c, 3 - z, jnp.where(z < c, z, jnp.where(c < 2, 3 - c, c)))

    def core_copy(g, i):
        to = flip(c, 1 + 2 * (1 - i))
        cols = cols_of(g)
        return remote(out1.at[to, :, cols], cbuf.at[i, :, cols], s_c.at[g, i], c_sem.at[g, i], cpart)

    def x_copy(g):
        cols = cols_of(g)
        return remote(out1.at[qx, :, cols], xbuf.at[:, cols], s_x.at[g], x_sem.at[g], xpart)

    def tick(step, carry):
        n = step - ag_first

        @pl.when((n >= 0) & (n < AG_N))
        def _():
            ag_step(n)

        m = step - rs_first

        @pl.when((m >= 0) & (m < 5 * CH))
        def _():
            rs_step(m)

        @pl.when(step == X_TICK)
        def _():
            got = flip(c, 2)
            arrived(n2buf.at[got], n2_sem.at[2])
            fwd = remote(n2buf.at[got], n2buf.at[got], s_n2.at[2], n2_sem.at[3], cpart)
            fwd.start()
            n2h[got], n2l[got] = split(n2buf[got])
            last = flip(c, 3)
            arrived(n2buf.at[last], n2_sem.at[3])
            n2h[last], n2l[last] = split(n2buf[last])

        @pl.when(step < 16)
        def _():
            turn_b(step)

        for i in range(2):
            e = (step - NEAR0) * 2 + i

            @pl.when((near == 1) & (e >= 0) & (e < CH))
            def _():
                near_step(e)

        e = step - ROOT0

        @pl.when((z == c) & (e >= 0) & (e < CH))
        def _():
            root_step(e)

        q = step - Y0

        @pl.when((q >= 0) & (q < 3 * CH))
        def _():
            y_step(q)

        @pl.when(sum(jnp.where(step == a, 1, 0) for a in A_TICK) > 0)
        def _():
            turn_a(sum(jnp.where(step >= a, 1, 0) for a in A_TICK) - 1)

        for g in range(2):
            end_a = A_TICK[8 * g + 7] + 1

            @pl.when(step == end_a)
            def _():
                core_copy(g, 0).start()
                core_copy(g, 1).start()

            @pl.when(step == end_a + 1)
            def _():
                cols = cols_of(g)
                core_copy(g, 0).wait_recv()
                out1[qx, :, cols] += cbuf[0, :, cols]
                x_copy(g).start()
                core_copy(g, 1).wait_recv()
                out1[c, :, cols] += cbuf[1, :, cols]

        return carry

    last_tick = max(RS0 + 3 * RS_LAG + 5 * CH, AG_N + 3 * AG_LAG, A_TICK[15] + 3, Y0 + 3 * CH)
    lax.fori_loop(0, last_tick, tick, 0)

    for g in range(2):
        x_copy(g).wait_recv()
    y1_out[...] = out1[c] + xbuf[...]
    for ch in range(CH):
        part = pl.ds(ch * wr, wr)
        arrived(y2buf.at[part], y2_sem.at[ch])
    y2_out[...] = y2buf[...]

    def sent(ref, sem):
        pltpu.make_async_copy(ref, ref, sem).wait()

    whole = n2buf.at[0]
    for i in range(3):
        sent(whole, s_n2.at[i])
    for g in range(2):
        for i in range(2):
            core_copy(g, i).wait_send()
        x_copy(g).wait_send()
    bit = n1buf.at[(0, *chunk_of(0))]
    wbit = out2.at[0, pl.ds(0, wr)]

    @pl.loop(0, AG_N)
    def _(n):
        o, t, ch = ag_of(n)

        @pl.when((z >= c) & (z < 3))
        def _():
            sent(bit, s_up.at[n])

        @pl.when((z <= c) & (z > 0))
        def _():
            sent(bit, s_dn.at[n])

        @pl.when(goes_y(o, t))
        def _():
            sent(bit, s_y.at[t, ch])

    @pl.loop(0, 5 * CH)
    def _(n):
        s, ch = n // CH, n % CH

        @pl.when((z != c) | (pick(RS_O, s) == 1) | (pick(RS_T, s) > 0))
        def _():
            sent(wbit, s_line.at[n])

        @pl.when(s < 3)
        def _():
            sent(wbit, s_ry.at[s + 1, ch])

        @pl.when((s == 0) & (c != z))
        def _():
            sent(bit, s_root.at[ch])


def panels(trailing, f1, inv1, f2, inv2, list1, list2):
    piece, width = f1.shape
    dma = pltpu.SemaphoreType.DMA
    vm = pltpu.VMEM
    scratch = [
        vm((8, piece, width), F32),
        vm((4, width, piece), F32),
        vm((4, width, piece), BF16),
        vm((4, width, piece), BF16),
        vm((4, piece, width), F32),
        vm((8, width, piece), F32),
        vm((5, width, piece), F32),
        vm((5, width, piece), F32),
        vm((4, width, piece), F32),
        vm((width, piece), F32),
        vm((width, piece), F32),
        vm((2, 2 * piece, piece), F32),
        vm((piece, width // 2), BF16),
        vm((piece, width // 2), BF16),
        vm((2, piece, width), F32),
        vm((piece, width), F32),
        dma((4,)), dma((CH,)), dma((8, CH)), dma((4,)), dma((5 * CH,)), dma((5 * CH,)), dma((4, CH)), dma((CH,)), dma((2,)), dma((2, 2)), dma((2,)),
        dma((AG_N,)), dma((AG_N,)), dma((4, CH)), dma((CH,)), dma((3,)), dma((4, CH)), dma((5 * CH,)), dma((2, 2)), dma((2,)),
    ]
    anyspace = pl.BlockSpec(memory_space=pl.ANY)
    inv = pl.BlockSpec(memory_space=pltpu.VMEM)
    return pl.pallas_call(
        panels_kernel,
        out_shape=(
            jax.ShapeDtypeStruct((piece, width), F32),
            jax.ShapeDtypeStruct((width, piece), F32),
        )
        * 2,
        in_specs=[anyspace] * 5 + [inv, inv],
        out_specs=(inv,) * 4,
        scratch_shapes=scratch,
        compiler_params=pltpu.CompilerParams(
            collective_id=0, has_side_effects=True, vmem_limit_bytes=63 * 2**20
        ),
        name="panels",
    )(trailing, f1, inv1, f2, inv2, list1, list2)


def finish_kernel(
    y1, y2t, n1, n2t, list1, list2, inv1, inv2, f_top,
    col1, diag1, col2, cross2, diag2,
    part0, part1, part2, sum0, sum1, sum2, top, top_t, square1, square2,
    acc, got1, got2, got3, got4, recv, send, z_recv, z_send, z_back, z_out,
):
    parts, outs = (part0, part1, part2), (sum0, sum1, sum2)
    r, c = lax.axis_index("row"), lax.axis_index("col")
    z, y, x, k = r // 2, r % 2, c // 2, c % 2
    ypart = (r + 1 - 2 * y, c)
    cpart = (r, flip(c, 1))
    xpart = (r, flip(c, 2))
    rows, cols = parts[0].shape
    h1, h2, h3, h4 = rows // 2, rows // 4, rows // 8, rows // 32
    side = [pl.ds(0, cols // 2), pl.ds(cols // 2, cols // 2)]
    first, second = (x, y), (y, x)
    one, two = (xpart, ypart), (ypart, xpart)
    base = k * h1
    at1 = [first[i] * h2 for i in (0, 1)]
    at2 = [at1[i] + second[i] * h3 for i in (0, 1)]
    line = [(lax.rem(r + 2 * d, 8), c) for d in (1, 2, 3)]

    def remote(src, dst, s_sem, r_sem, to):
        return pltpu.make_async_remote_copy(
            src_ref=src, dst_ref=dst, send_sem=s_sem, recv_sem=r_sem, device_id=to, device_id_type=MESH
        )

    def span(start, size):
        return pl.ds(pl.multiple_of(start, size), size)

    bar = pltpu.get_barrier_semaphore()
    for to in [ypart, cpart, xpart] + line:
        pl.semaphore_signal(bar, inc=1, device_id=to, device_id_type=MESH)
    pl.semaphore_wait(bar, 6)

    def copies(m, stage):
        if stage == 0:
            return [remote(parts[m].at[span((1 - k) * h1, h1)], got1.at[m], send.at[m, 0, 0], recv.at[m, 0, 0], cpart)]
        if stage == 1:
            return [
                remote(acc.at[m, span((1 - first[i]) * h2, h2), side[i]], got2.at[m, i], send.at[m, 1, i], recv.at[m, 1, i], one[i])
                for i in (0, 1)
            ]
        if stage == 2:
            return [
                remote(
                    acc.at[m, span(at1[i] + (1 - second[i]) * h3, h3), side[i]],
                    got3.at[m, i], send.at[m, 2, i], recv.at[m, 2, i], two[i],
                )
                for i in (0, 1)
            ]
        if stage == 3:
            return [
                remote(
                    acc.at[m, span(at2[i] + lax.rem(z + d, 4) * h4, h4), side[i]],
                    got4.at[m, d - 1, i], z_send.at[m, d - 1, i], z_recv.at[m, d - 1, i], line[d - 1],
                )
                for d in (1, 2, 3)
                for i in (0, 1)
            ]
        if stage == 4:
            places = [outs[m].at[span(base + at2[i] + z * h4, h4), side[i]] for i in (0, 1)]
            return [
                remote(places[i], places[i], z_out.at[m, d - 1, i], z_back.at[m, d - 1, i], line[d - 1])
                for d in (1, 2, 3)
                for i in (0, 1)
            ]
        if stage == 7:
            place = outs[m].at[span(base, h1)]
            return [remote(place, place, send.at[m, 5, 0], recv.at[m, 5, 0], cpart)]
        to = (two, one)[stage - 5]
        size, at = ((h3, at2), (h2, at1))[stage - 5]
        places = [outs[m].at[span(base + at[i], size), side[i]] for i in (0, 1)]
        return [remote(places[i], places[i], send.at[m, stage - 2, i], recv.at[m, stage - 2, i], to[i]) for i in (0, 1)]

    def take(m, stage):
        for cp in copies(m, stage):
            cp.wait_recv()
        if stage == 0:
            acc[m] = parts[m][span(base, h1)] + got1[m]
        for i in (0, 1):
            if stage == 1:
                acc[m, span(at1[i], h2), side[i]] += got2[m, i]
            if stage == 2:
                acc[m, span(at2[i], h3), side[i]] += got3[m, i]
            if stage == 3:
                mine = acc[m, span(at2[i] + z * h4, h4), side[i]] + got4[m, 0, i] + (got4[m, 1, i] + got4[m, 2, i])
                outs[m][span(base + at2[i] + z * h4, h4), side[i]] = mine

    def make(m):
        if m == 0:
            col1[...] = -row_mask(list1, rows) * y1[...]
            part0[...] = mm3(n1[...].T, col1[...])
        if m == 1:
            part1[...] = mm3(n2t[...], col1[...])
            top[...] = mm3(f_top[...], inv2[...])
        if m == 2:
            col2[...] = -row_mask(list2, rows) * (y2t[...].T + mm3(col1[...], top[...]))
            part2[...] = mm3(n2t[...], col2[...])

    for step in range(8 + 3):
        if step == 3:
            square1[...] = mm3(inv1[...].T, inv1[...])
        if step == 4:
            square2[...] = mm3(inv2[...].T, inv2[...])
        if step == 5:
            top_t[...] = top[...].T
        for m in range(3):
            stage = step - m
            if stage == 0:
                make(m)
            if 1 <= stage <= 8:
                take(m, stage - 1)
            if 0 <= stage < 8:
                for cp in copies(m, stage):
                    cp.start()
        if step == 9:
            diag1[...] = square1[...] - sum0[...]
            cross2[...] = -(mm3(diag1[...], top[...]) + sum1[...].T)
            square2[...] -= mm3(top_t[...], cross2[...])
    diag2[...] = square2[...] - sum2[...]
    for m in range(3):
        for stage in range(8):
            for cp in copies(m, stage):
                cp.wait_send()


def finish(y1, y2t, n1, n2t, list1, list2, inv1, inv2, f_top):
    rows, cols = y1.shape
    w = cols // 2
    dma = pltpu.SemaphoreType.DMA
    vm = pltpu.VMEM
    inv = pl.BlockSpec(memory_space=pltpu.VMEM)
    return pl.pallas_call(
        finish_kernel,
        out_shape=(jax.ShapeDtypeStruct((rows, cols), F32),) * 5,
        in_specs=[inv] * 9,
        out_specs=(inv,) * 5,
        scratch_shapes=[
            *[vm((rows, cols), F32)] * 10,
            vm((3, rows // 2, cols), F32),
            vm((3, rows // 2, cols), F32),
            vm((3, 2, rows // 4, w), F32),
            vm((3, 2, rows // 8, w), F32),
            vm((3, 3, 2, rows // 32, w), F32),
            dma((3, 6, 2)), dma((3, 6, 2)),
            dma((3, 3, 2)), dma((3, 3, 2)), dma((3, 3, 2)), dma((3, 3, 2)),
        ],
        compiler_params=pltpu.CompilerParams(
            collective_id=1, has_side_effects=True, vmem_limit_bytes=60 * 2**20
        ),
        name="finish",
    )(y1, y2t, n1, n2t, list1, list2, inv1, inv2, f_top)


def hand_over_kernel(*refs):
    for i in range(5):
        refs[5 + i][...] = refs[i][...]


def hand_over(arrays):
    inv = pl.BlockSpec(memory_space=pltpu.VMEM)
    return pl.pallas_call(
        hand_over_kernel,
        out_shape=tuple(jax.ShapeDtypeStruct(a.shape, a.dtype) for a in arrays),
        in_specs=[inv] * 5,
        out_specs=(inv,) * 5,
        name="hand_over",
    )(*arrays)


def column_panel(normal):
    rows, cols = lax.axis_size("row"), lax.axis_size("col")
    moves = [(p, (p % rows) * cols + p // rows) for p in range(rows * cols)]
    piece = lax.ppermute(normal, ("row", "col"), moves)
    return lax.all_gather(piece, "row", axis=0, tiled=True)


def sweep(trailing, col_block):
    part = big_product(trailing, col_block)
    return lax.psum_scatter(part, "col", scatter_dimension=0, tiled=True)


def body(
    special,
    trailing,
    factor_one,
    inverse_one,
    factor_two_top,
    factor_two,
    inverse_two,
    structure_one,
    structure_two,
):
    piece_rows = factor_one.shape[0]
    if special and piece_rows == factor_one.shape[1]:
        lists = (structure_one[None, :], structure_two[None, :])
        sums = panels(trailing, factor_one, inverse_one, factor_two, inverse_two, *lists)
        return hand_over(finish(*sums, *lists, inverse_one, inverse_two, factor_two_top))
    row_index = lax.axis_index("row")
    col_index = lax.axis_index("col")
    first_row = (row_index * lax.axis_size("col") + col_index) * piece_rows
    mask_one = block_flags(structure_one, first_row, piece_rows)
    mask_two = block_flags(structure_two, first_row, piece_rows)
    normal_one = mask_one * product(factor_one, inverse_one)
    normal_two = mask_two * product(factor_two, inverse_two)
    normal_top = product(factor_two_top, inverse_two)
    column_one = -mask_one * sweep(trailing, column_panel(normal_one))
    column_two = -mask_two * (sweep(trailing, column_panel(normal_two)) + product(column_one, normal_top))
    parts = (
        product(normal_one.T, column_one),
        product(column_one.T, normal_two),
        product(normal_two.T, column_two),
    )
    first, cross, second = lax.psum(parts, ("row", "col"))
    diagonal_one = product(inverse_one.T, inverse_one) - first
    cross_two = -(product(diagonal_one, normal_top) + cross)
    diagonal_two = product(inverse_two.T, inverse_two) - product(normal_top.T, cross_two) - second
    return (column_one, diagonal_one, column_two, cross_two, diagonal_two)


def solution(mesh):
    special = mesh.shape["row"] == 8 and mesh.shape["col"] == 4
    return jax.shard_map(
        functools.partial(body, special),
        mesh=mesh,
        in_specs=(
            P("row", "col"),
            P(("row", "col"), None),
            P(),
            P(),
            P(("row", "col"), None),
            P(),
            P(),
            P(),
        ),
        out_specs=(P(("row", "col"), None), P(), P(("row", "col"), None), P(), P()),
        check_vma=False,
    )
```

```python
import functools

import jax
import jax.numpy as jnp
from jax import lax
from jax.experimental import pallas as pl
from jax.experimental.pallas import tpu as pltpu
from jax.sharding import PartitionSpec as P

BLK = 128
MESH = pl.DeviceIdType.MESH
CH = 8
AG_LAG = 1
RS_LAG = 5
RS0 = 10
Y0 = 16
NEAR0 = 16
ROOT0 = 41
X_TICK = 8
AG_O, AG_T = (0, 0, 0, 0, 1, 1), (1, 0, 2, 3, 0, 1)
RS_O, RS_T = (1, 0, 0, 0, 0), (0, 3, 2, 0, 1)
B_O, B_T = (1, 1, 1, 0, 1, 0, 0, 0), (0, 1, 3, 3, 2, 2, 1, 0)
A_O, A_T = (0, 0, 0, 0, 1, 1, 1, 1), (1, 0, 2, 3, 0, 2, 3, 1)
Y_T = (3, 2, 1)
QR = CH // 2
AG_N = 2 * len(AG_T) * QR
A_TICK = (20, 21, 22, 23, 24, 25, 26, 27, 31, 35, 39, 43, 47, 48, 49, 51)
F32 = jnp.float32
BF16 = jnp.bfloat16


def product(left, right):
    return jnp.dot(left, right, precision=lax.Precision.HIGHEST, preferred_element_type=jnp.float32)


def big_product(left, right):
    return jnp.dot(left, right, precision=lax.Precision.HIGH, preferred_element_type=jnp.float32)


def block_flags(structure, first_row, count):
    blocks = (first_row + jnp.arange(count, dtype=jnp.int32)) // BLK
    hits = jnp.any(blocks[:, None] == structure[None, :], axis=1)
    return hits.astype(jnp.float32)[:, None]


def split(value):
    high = value.astype(BF16)
    return high, (value - high.astype(F32)).astype(BF16)


def mm(left, right):
    return jnp.dot(left, right, preferred_element_type=F32)


def mm3(left, right):
    lh, ll = split(left)
    rh, rl = split(right)
    return mm(lh, rh) + (mm(ll, rh) + mm(lh, rl))


def flip(c, t):
    return ((c // 2 + t // 2) % 2) * 2 + (c % 2 + t % 2) % 2


def pick(table, index):
    return sum(jnp.where(index == i, v, 0) for i, v in enumerate(table) if v)


def row_mask(blocks, piece):
    first = (lax.axis_index("row") * lax.axis_size("col") + lax.axis_index("col")) * piece
    listed = blocks[...]
    rows = first + lax.broadcasted_iota(jnp.int32, (piece, listed.shape[1]), 0)
    hits = jnp.where(rows // BLK == listed, 1.0, 0.0)
    return jnp.max(hits, axis=1, keepdims=True)


def panels_kernel(
    trail, f1, inv1, f2, inv2, list1, list2, y1_out, y2_out, n1_in, n2_in,
    n1buf, n2buf, n2h, n2l, out1, out2, rsu, rsd, rsy, rsn, y2buf, tbuf, n1h, n1l, cbuf, xbuf,
    f_sem, near_sem, ag_sem, n2_sem, up_sem, dn_sem, ry_sem, y2_sem, t_sem, c_sem, x_sem,
    s_up, s_dn, s_y, s_root, s_n2, s_ry, s_line, s_c, s_x,
):
    r, c = lax.axis_index("row"), lax.axis_index("col")
    z, y, x, k = r // 2, r % 2, c // 2, c % 2
    piece = n1_in.shape[0]
    width = n1_in.shape[1]
    cr, gw = piece // QR, width // 2
    wr = n2_in.shape[0] // CH
    ypart = (r + 1 - 2 * y, c)
    cpart = (r, flip(c, 1))
    xpart = (r, flip(c, 2))
    above = (lax.rem(r + 2, 8), c)
    below = (lax.rem(r + 6, 8), c)
    near = jnp.where((z // 2 == x) & (z != c), 1, 0)
    dist = jnp.where(z > c, z - c, c - z)

    def remote(src, dst, send, recv, to):
        return pltpu.make_async_remote_copy(
            src_ref=src, dst_ref=dst, send_sem=send, recv_sem=recv, device_id=to, device_id_type=MESH
        )

    def cols_of(g):
        return pl.ds(pl.multiple_of(g * gw, gw), gw)

    def chunk_of(ch):
        return pl.ds(pl.multiple_of((ch % QR) * cr, cr), cr), cols_of(ch // QR)

    def arrived(ref, sem):
        pltpu.make_async_copy(ref, ref, sem).wait()

    bar = pltpu.get_barrier_semaphore()
    for to in (ypart, cpart, xpart, (r, flip(c, 3))):
        pl.semaphore_signal(bar, inc=1, device_id=to, device_id_type=MESH)

    @pl.when(z < 3)
    def _():
        pl.semaphore_signal(bar, inc=1, device_id=above, device_id_type=MESH)

    @pl.when(z > 0)
    def _():
        pl.semaphore_signal(bar, inc=1, device_id=below, device_id_type=MESH)

    def tile_of(u):
        isa = jnp.where(u >= 16, 1, 0)
        w = (u - 16) * isa
        pb, pa = u % 8, (w // 2) % 8
        t = isa * pick(A_T, pa) + (1 - isa) * pick(B_T, pb)
        o = isa * pick(A_O, pa) + (1 - isa) * pick(B_O, pb)
        h = isa * (w % 2) + (1 - isa) * ((x + u // 8) % 2)
        return ((y + o) % 2) * 4 + flip(c, t), h, t, o

    half = 2 * piece

    def fetch(u):
        j, h, _, _ = tile_of(u)
        rows = pl.ds(pl.multiple_of(h * half, half), half)
        cols = pl.ds(pl.multiple_of(j * piece, piece), piece)
        return pltpu.make_async_copy(trail.at[rows, cols], tbuf.at[u % 2], t_sem.at[u % 2])

    fetch(0).start()
    loads = [pltpu.make_async_copy(a, out2.at[i], f_sem.at[i]) for i, a in enumerate((f2, inv2, f1, inv1))]
    for cp in loads:
        cp.start()
    loads[0].wait()
    loads[1].wait()
    cut = width // 2
    left, right = pl.ds(0, cut), pl.ds(cut, cut)
    listed = row_mask(list2, piece)

    def send_half(rows):
        remote(n2_in.at[rows], n2buf.at[c, rows], s_n2.at[0], n2_sem.at[2], xpart).start()
        remote(n2_in.at[rows], n2buf.at[c, rows], s_n2.at[1], n2_sem.at[1], cpart).start()
        pltpu.make_async_copy(n2_in.at[rows], n2buf.at[c, rows], n2_sem.at[0]).start()

    n2_in[right] = (listed * mm3(out2[0, :, right], out2[1, right, right])).T

    pl.semaphore_wait(bar, 4 + (z + 2) // 3 + (5 - z) // 3)
    send_half(right)
    n2_in[left] = (listed * mm3(out2[0], out2[1, :, left])).T
    send_half(left)

    loads[2].wait()
    loads[3].wait()
    listed = row_mask(list1, piece)
    n1_in[:, left] = listed * mm3(out2[2], out2[3, :, left])
    n1_in[:, right] = listed * mm3(out2[2, :, right], out2[3, right, right])
    here = y * 4 + c
    for ch in range(CH):
        part = chunk_of(ch)

        @pl.when(c == z)
        def _():
            pltpu.make_async_copy(n1_in.at[part], n1buf.at[(here, *part)], ag_sem.at[here, ch]).start()

        @pl.when(c != z)
        def _():
            remote(n1_in.at[part], n1buf.at[(here, *part)], s_root.at[ch], ag_sem.at[here, ch], (r, z)).start()

    arrived(n2buf.at[c], n2_sem.at[0])
    arrived(n2buf.at[flip(c, 1)], n2_sem.at[1])
    for t in range(2):
        q = flip(c, t)
        n2h[q], n2l[q] = split(n2buf[q])

    def ag_of(n):
        g, s, i = n // (len(AG_T) * QR), (n // QR) % len(AG_T), n % QR
        return pick(AG_O, s), pick(AG_T, s), g * QR + i

    def goes_y(o, t):
        return (o == 0) & ((t > 1) | (z == c))

    def ag_step(n):
        o, t, ch = ag_of(n)
        j = ((y + o) % 2) * 4 + flip(c, t)
        chunk = n1buf.at[(j, *chunk_of(ch))]
        arrived(chunk, ag_sem.at[j, ch])

        @pl.when((z >= c) & (z < 3))
        def _():
            remote(chunk, chunk, s_up.at[n], ag_sem.at[j, ch], above).start()

        @pl.when((z <= c) & (z > 0))
        def _():
            remote(chunk, chunk, s_dn.at[n], ag_sem.at[j, ch], below).start()

        @pl.when(goes_y(o, t))
        def _():
            remote(chunk, chunk, s_y.at[t, ch], ag_sem.at[j, ch], ypart).start()

    def rs_step(n):
        s, ch = n // CH, n % CH
        o, t = pick(RS_O, s), pick(RS_T, s)
        j = ((y + o) % 2) * 4 + flip(c, t)
        part = pl.ds(pl.multiple_of(ch * wr, wr), wr)
        chunk = out2.at[j, part]

        @pl.when((z >= c) & (z < 3))
        def _():
            arrived(rsu.at[s, part], up_sem.at[n])
            chunk[...] += rsu[s, part]

        @pl.when((z <= c) & (z > 0))
        def _():
            arrived(rsd.at[s, part], dn_sem.at[n])
            chunk[...] += rsd[s, part]

        @pl.when((o == 0) & ((t > 1) | (z == c) | ((t == 1) & (near == 0))))
        def _():
            arrived(rsy.at[t, part], ry_sem.at[t, ch])
            chunk[...] += rsy[t, part]

        @pl.when(z > c)
        def _():
            remote(chunk, rsu.at[s, part], s_line.at[n], up_sem.at[n], below).start()

        @pl.when(z < c)
        def _():
            remote(chunk, rsd.at[s, part], s_line.at[n], dn_sem.at[n], above).start()

        @pl.when((z == c) & (o == 1))
        def _():
            remote(chunk, rsy.at[0, part], s_line.at[n], ry_sem.at[0, ch], ypart).start()

        @pl.when((z == c) & (o == 0) & (t > 0))
        def _():
            remote(chunk, y2buf.at[part], s_line.at[n], y2_sem.at[ch], (r, flip(c, t))).start()

        @pl.when((z == c) & (o == 0) & (t == 0))
        def _():
            pltpu.make_async_copy(chunk, y2buf.at[part], y2_sem.at[ch]).start()

    def turn_b(u):
        j, h, t, o = tile_of(u)
        fetch(u).wait()
        fetch(u + 1).start()

        @pl.loop(0, 2)
        def _(i):
            rows = pl.ds(pl.multiple_of(i * piece, piece), piece)
            th, tl = split(tbuf[u % 2, rows])
            q = 2 * h + i
            add = mm(n2h[q], th) + (mm(n2l[q], th) + mm(n2h[q], tl))

            @pl.when((u < 8) & (i == 0))
            def _():
                out2[j] = add

            @pl.when((u >= 8) | (i == 1))
            def _():
                out2[j] += add

    def y_step(q):
        t, ch = pick(Y_T, q // CH), q % CH
        part = pl.ds(pl.multiple_of(ch * wr, wr), wr)
        j = ((y + 1) % 2) * 4 + flip(c, t)

        @pl.when((t > 1) | ((near == 0) & (z != c)))
        def _():
            remote(out2.at[j, part], rsy.at[t, part], s_ry.at[t, ch], ry_sem.at[t, ch], ypart).start()

    j_near = ((y + 1) % 2) * 4 + flip(c, 1)

    def near_step(ch):
        part = pl.ds(pl.multiple_of(ch * wr, wr), wr)
        remote(out2.at[j_near, part], rsn.at[part], s_ry.at[1, ch], near_sem.at[ch], (lax.rem(r + jnp.where(z < c, 2, 6), 8), c)).start()

    def root_step(ch):
        part = pl.ds(pl.multiple_of(ch * wr, wr), wr)
        arrived(rsn.at[part], near_sem.at[ch])
        out2[j_near, part] += rsn[part]
        remote(out2.at[j_near, part], rsy.at[1, part], s_ry.at[1, ch], ry_sem.at[1, ch], ypart).start()

    def turn_a(turn):
        g = turn // 8
        cols = cols_of(g)
        j, _, t, o = tile_of(16 + 2 * turn)

        @pl.when((o == 1) & (t >= 2))
        def _():
            for i in range(QR):
                ch = g * QR + i
                arrived(n1buf.at[(j, *chunk_of(ch))], ag_sem.at[j, ch])

        n1h[...], n1l[...] = split(n1buf[j, :, cols])

        @pl.loop(0, 2)
        def _(h):
            u = 16 + 2 * turn + h
            fetch(u).wait()

            @pl.when(u < 47)
            def _():
                fetch(u + 1).start()

            @pl.loop(0, 2)
            def _(i):
                rows = pl.ds(pl.multiple_of(i * piece, piece), piece)
                th, tl = split(tbuf[u % 2, rows])
                add = mm(th, n1h[...]) + (mm(th, n1l[...]) + mm(tl, n1h[...]))
                q = 2 * h + i

                @pl.when(turn % 8 == 0)
                def _():
                    out1[q, :, cols] = add

                @pl.when(turn % 8 > 0)
                def _():
                    out1[q, :, cols] += add

    qx = flip(c, 2)
    ag_first = AG_LAG * dist
    rs_first = RS0 + RS_LAG * jnp.where(z > c, 3 - z, jnp.where(z < c, z, jnp.where(c < 2, 3 - c, c)))

    def core_copy(g, i):
        to = flip(c, 1 + 2 * (1 - i))
        cols = cols_of(g)
        return remote(out1.at[to, :, cols], cbuf.at[i, :, cols], s_c.at[g, i], c_sem.at[g, i], cpart)

    def x_copy(g):
        cols = cols_of(g)
        return remote(out1.at[qx, :, cols], xbuf.at[:, cols], s_x.at[g], x_sem.at[g], xpart)

    def tick(step, carry):
        n = step - ag_first

        @pl.when((n >= 0) & (n < AG_N))
        def _():
            ag_step(n)

        m = step - rs_first

        @pl.when((m >= 0) & (m < 5 * CH))
        def _():
            rs_step(m)

        @pl.when(step == X_TICK)
        def _():
            got = flip(c, 2)
            arrived(n2buf.at[got], n2_sem.at[2])
            fwd = remote(n2buf.at[got], n2buf.at[got], s_n2.at[2], n2_sem.at[3], cpart)
            fwd.start()
            n2h[got], n2l[got] = split(n2buf[got])
            last = flip(c, 3)
            arrived(n2buf.at[last], n2_sem.at[3])
            n2h[last], n2l[last] = split(n2buf[last])

        @pl.when(step < 16)
        def _():
            turn_b(step)

        for i in range(2):
            e = (step - NEAR0) * 2 + i

            @pl.when((near == 1) & (e >= 0) & (e < CH))
            def _():
                near_step(e)

        e = step - ROOT0

        @pl.when((z == c) & (e >= 0) & (e < CH))
        def _():
            root_step(e)

        q = step - Y0

        @pl.when((q >= 0) & (q < 3 * CH))
        def _():
            y_step(q)

        @pl.when(sum(jnp.where(step == a, 1, 0) for a in A_TICK) > 0)
        def _():
            turn_a(sum(jnp.where(step >= a, 1, 0) for a in A_TICK) - 1)

        for g in range(2):
            end_a = A_TICK[8 * g + 7] + 1

            @pl.when(step == end_a)
            def _():
                core_copy(g, 0).start()
                core_copy(g, 1).start()

            @pl.when(step == end_a + 1)
            def _():
                cols = cols_of(g)
                core_copy(g, 0).wait_recv()
                out1[qx, :, cols] += cbuf[0, :, cols]
                x_copy(g).start()
                core_copy(g, 1).wait_recv()
                out1[c, :, cols] += cbuf[1, :, cols]

        return carry

    last_tick = max(RS0 + 3 * RS_LAG + 5 * CH, AG_N + 3 * AG_LAG, A_TICK[15] + 3, Y0 + 3 * CH)
    lax.fori_loop(0, last_tick, tick, 0)

    for g in range(2):
        x_copy(g).wait_recv()
    y1_out[...] = out1[c] + xbuf[...]
    for ch in range(CH):
        part = pl.ds(ch * wr, wr)
        arrived(y2buf.at[part], y2_sem.at[ch])
    y2_out[...] = y2buf[...]

    def sent(ref, sem):
        pltpu.make_async_copy(ref, ref, sem).wait()

    whole = n2buf.at[0]
    for i in range(3):
        sent(whole, s_n2.at[i])
    for g in range(2):
        for i in range(2):
            core_copy(g, i).wait_send()
        x_copy(g).wait_send()
    bit = n1buf.at[(0, *chunk_of(0))]
    wbit = out2.at[0, pl.ds(0, wr)]

    @pl.loop(0, AG_N)
    def _(n):
        o, t, ch = ag_of(n)

        @pl.when((z >= c) & (z < 3))
        def _():
            sent(bit, s_up.at[n])

        @pl.when((z <= c) & (z > 0))
        def _():
            sent(bit, s_dn.at[n])

        @pl.when(goes_y(o, t))
        def _():
            sent(bit, s_y.at[t, ch])

    @pl.loop(0, 5 * CH)
    def _(n):
        s, ch = n // CH, n % CH

        @pl.when((z != c) | (pick(RS_O, s) == 1) | (pick(RS_T, s) > 0))
        def _():
            sent(wbit, s_line.at[n])

        @pl.when(s < 3)
        def _():
            sent(wbit, s_ry.at[s + 1, ch])

        @pl.when((s == 0) & (c != z))
        def _():
            sent(bit, s_root.at[ch])


def panels(trailing, f1, inv1, f2, inv2, list1, list2):
    piece, width = f1.shape
    dma = pltpu.SemaphoreType.DMA
    vm = pltpu.VMEM
    scratch = [
        vm((8, piece, width), F32),
        vm((4, width, piece), F32),
        vm((4, width, piece), BF16),
        vm((4, width, piece), BF16),
        vm((4, piece, width), F32),
        vm((8, width, piece), F32),
        vm((5, width, piece), F32),
        vm((5, width, piece), F32),
        vm((4, width, piece), F32),
        vm((width, piece), F32),
        vm((width, piece), F32),
        vm((2, 2 * piece, piece), F32),
        vm((piece, width // 2), BF16),
        vm((piece, width // 2), BF16),
        vm((2, piece, width), F32),
        vm((piece, width), F32),
        dma((4,)), dma((CH,)), dma((8, CH)), dma((4,)), dma((5 * CH,)), dma((5 * CH,)), dma((4, CH)), dma((CH,)), dma((2,)), dma((2, 2)), dma((2,)),
        dma((AG_N,)), dma((AG_N,)), dma((4, CH)), dma((CH,)), dma((3,)), dma((4, CH)), dma((5 * CH,)), dma((2, 2)), dma((2,)),
    ]
    anyspace = pl.BlockSpec(memory_space=pl.ANY)
    inv = pl.BlockSpec(memory_space=pltpu.VMEM)
    return pl.pallas_call(
        panels_kernel,
        out_shape=(
            jax.ShapeDtypeStruct((piece, width), F32),
            jax.ShapeDtypeStruct((width, piece), F32),
        )
        * 2,
        in_specs=[anyspace] * 5 + [inv, inv],
        out_specs=(inv,) * 4,
        scratch_shapes=scratch,
        compiler_params=pltpu.CompilerParams(
            collective_id=0, has_side_effects=True, vmem_limit_bytes=63 * 2**20
        ),
        name="panels",
    )(trailing, f1, inv1, f2, inv2, list1, list2)


def finish_kernel(
    y1, y2t, n1, n2t, list1, list2, inv1, inv2, f_top,
    col1, diag1, col2, cross2, diag2,
    part0, part1, part2, sum0, sum1, sum2, top, top_t, square1, square2,
    acc, got1, got2, got3, got4, recv, send, z_recv, z_send, z_back, z_out,
):
    parts, outs = (part0, part1, part2), (sum0, sum1, sum2)
    r, c = lax.axis_index("row"), lax.axis_index("col")
    z, y, x, k = r // 2, r % 2, c // 2, c % 2
    ypart = (r + 1 - 2 * y, c)
    cpart = (r, flip(c, 1))
    xpart = (r, flip(c, 2))
    rows, cols = part1.shape
    half, quarter = rows // 2, rows // 4
    zw = cols // 4
    first, second = (x, y), (y, x)
    one, two = (xpart, ypart), (ypart, xpart)
    h1, h2, h3 = ([parts[m].shape[0] // d for m in range(3)] for d in (2, 8, 16))
    base = [k * h1[m] for m in range(3)]
    at1 = [[i * (h1[m] // 2) + first[i] * h2[m] for i in (0, 1)] for m in range(3)]
    at2 = [[at1[m][i] + second[i] * h3[m] for i in (0, 1)] for m in range(3)]
    line = [(lax.rem(r + 2 * d, 8), c) for d in (1, 2, 3)]

    def remote(src, dst, s_sem, r_sem, to):
        return pltpu.make_async_remote_copy(
            src_ref=src, dst_ref=dst, send_sem=s_sem, recv_sem=r_sem, device_id=to, device_id_type=MESH
        )

    def span(start, size):
        return pl.ds(pl.multiple_of(start, 8), size)

    def side(zz):
        return pl.ds(pl.multiple_of(zz * zw, zw), zw)

    bar = pltpu.get_barrier_semaphore()
    for to in [ypart, cpart, xpart] + line:
        pl.semaphore_signal(bar, inc=1, device_id=to, device_id_type=MESH)
    pl.semaphore_wait(bar, 6)

    def copies(m, stage):
        if stage == 0:
            there = parts[m].at[span((1 - k) * h1[m], h1[m])]
            return [remote(there, got1.at[m, span(0, h1[m])], send.at[m, 0, 0], recv.at[m, 0, 0], cpart)]
        if stage == 1:
            return [
                remote(
                    acc.at[m, span(i * (h1[m] // 2) + (1 - first[i]) * h2[m], h2[m])],
                    got2.at[m, i, span(0, h2[m])], send.at[m, 1, i], recv.at[m, 1, i], one[i],
                )
                for i in (0, 1)
            ]
        if stage == 2:
            return [
                remote(
                    acc.at[m, span(at1[m][i] + (1 - second[i]) * h3[m], h3[m])],
                    got3.at[m, i, span(0, h3[m])], send.at[m, 2, i], recv.at[m, 2, i], two[i],
                )
                for i in (0, 1)
            ]
        if stage == 3:
            return [
                remote(
                    acc.at[m, span(at2[m][i], h3[m]), side(lax.rem(z + d, 4))],
                    got4.at[m, d - 1, i, span(0, h3[m])], z_send.at[m, d - 1, i], z_recv.at[m, d - 1, i], line[d - 1],
                )
                for d in (1, 2, 3)
                for i in (0, 1)
            ]
        if stage == 4:
            places = [outs[m].at[span(base[m] + at2[m][i], h3[m]), side(z)] for i in (0, 1)]
            return [
                remote(places[i], places[i], z_out.at[m, d - 1, i], z_back.at[m, d - 1, i], line[d - 1])
                for d in (1, 2, 3)
                for i in (0, 1)
            ]
        if stage == 7:
            place = outs[m].at[span(base[m], h1[m])]
            return [remote(place, place, send.at[m, 5, 0], recv.at[m, 5, 0], cpart)]
        to = (two, one)[stage - 5]
        size, at = ((h3[m], at2[m]), (h2[m], at1[m]))[stage - 5]
        places = [outs[m].at[span(base[m] + at[i], size)] for i in (0, 1)]
        return [remote(places[i], places[i], send.at[m, stage - 2, i], recv.at[m, stage - 2, i], to[i]) for i in (0, 1)]

    def take(m, stage):
        for cp in copies(m, stage):
            cp.wait_recv()
        if stage == 0:
            acc[m, span(0, h1[m])] = parts[m][span(base[m], h1[m])] + got1[m, span(0, h1[m])]
        for i in (0, 1):
            if stage == 1:
                acc[m, span(at1[m][i], h2[m])] += got2[m, i, span(0, h2[m])]
            if stage == 2:
                acc[m, span(at2[m][i], h3[m])] += got3[m, i, span(0, h3[m])]
            if stage == 3:
                got = [got4[m, d, i, span(0, h3[m])] for d in range(3)]
                mine = acc[m, span(at2[m][i], h3[m]), side(z)] + got[0] + (got[1] + got[2])
                outs[m][span(base[m] + at2[m][i], h3[m]), side(z)] = mine

    def pack(part, left, right):
        part[0:half] = mm3(left[0:half], right)
        last = mm3(left[half:rows], right[:, half:cols])
        part[half : half + quarter, 0:half] = last[0:quarter]
        part[half : half + quarter, half:cols] = last[quarter:half]

    def minus(out, value, total):
        out[0:half] = value[0:half] - total[0:half]
        out[half:rows, 0:half] = value[half:rows, 0:half] - total[0:half, half:cols].T
        out[half : half + quarter, half:cols] = value[half : half + quarter, half:cols] - total[half : half + quarter, 0:half]
        out[half + quarter : rows, half:cols] = value[half + quarter : rows, half:cols] - total[half : half + quarter, half:cols]

    def make(m):
        if m == 0:
            col1[...] = -row_mask(list1, rows) * y1[...]
            pack(part0, n1[...].T, col1[...])
        if m == 1:
            part1[...] = mm3(n2t[...], col1[...])
        if m == 2:
            col2[...] = -row_mask(list2, rows) * y2t[...].T
            pack(part2, n2t[...], col2[...])

    for step in range(8 + 3):
        if step == 3:
            top[...] = mm3(f_top[...], inv2[...])
            square1[...] = mm3(inv1[...].T, inv1[...])
        if step == 4:
            square2[...] = mm3(inv2[...].T, inv2[...])
        if step == 5:
            top_t[...] = top[...].T
        if step == 6:
            col2[...] -= row_mask(list2, rows) * mm3(col1[...], top[...])
        for m in range(3):
            stage = step - m
            if stage == 0:
                make(m)
            if 1 <= stage <= 8:
                take(m, stage - 1)
            if 0 <= stage < 8:
                for cp in copies(m, stage):
                    cp.start()
        if step == 9:
            minus(diag1, square1, sum0)
            cross2[...] = -(mm3(diag1[...], top[...]) + sum1[...].T)
            square2[...] += mm3(sum1[...], top[...]) - mm3(top_t[...], cross2[...])
    minus(diag2, square2, sum2)
    for m in range(3):
        for stage in range(8):
            for cp in copies(m, stage):
                cp.wait_send()


def finish(y1, y2t, n1, n2t, list1, list2, inv1, inv2, f_top):
    rows, cols = y1.shape
    dma = pltpu.SemaphoreType.DMA
    vm = pltpu.VMEM
    inv = pl.BlockSpec(memory_space=pltpu.VMEM)
    return pl.pallas_call(
        finish_kernel,
        out_shape=(jax.ShapeDtypeStruct((rows, cols), F32),) * 5,
        in_specs=[inv] * 9,
        out_specs=(inv,) * 5,
        scratch_shapes=[
            vm((3 * rows // 4, cols), F32), vm((rows, cols), F32), vm((3 * rows // 4, cols), F32),
            vm((3 * rows // 4, cols), F32), vm((rows, cols), F32), vm((3 * rows // 4, cols), F32),
            *[vm((rows, cols), F32)] * 4,
            vm((3, rows // 2, cols), F32),
            vm((3, rows // 2, cols), F32),
            vm((3, 2, rows // 8, cols), F32),
            vm((3, 2, rows // 16, cols), F32),
            vm((3, 3, 2, rows // 16, cols // 4), F32),
            dma((3, 6, 2)), dma((3, 6, 2)),
            dma((3, 3, 2)), dma((3, 3, 2)), dma((3, 3, 2)), dma((3, 3, 2)),
        ],
        compiler_params=pltpu.CompilerParams(
            collective_id=1, has_side_effects=True, vmem_limit_bytes=60 * 2**20
        ),
        name="finish",
    )(y1, y2t, n1, n2t, list1, list2, inv1, inv2, f_top)


def hand_over_kernel(*refs):
    for i in range(5):
        refs[5 + i][...] = refs[i][...]


def hand_over(arrays):
    inv = pl.BlockSpec(memory_space=pltpu.VMEM)
    return pl.pallas_call(
        hand_over_kernel,
        out_shape=tuple(jax.ShapeDtypeStruct(a.shape, a.dtype) for a in arrays),
        in_specs=[inv] * 5,
        out_specs=(inv,) * 5,
        name="hand_over",
    )(*arrays)


def column_panel(normal):
    rows, cols = lax.axis_size("row"), lax.axis_size("col")
    moves = [(p, (p % rows) * cols + p // rows) for p in range(rows * cols)]
    piece = lax.ppermute(normal, ("row", "col"), moves)
    return lax.all_gather(piece, "row", axis=0, tiled=True)


def sweep(trailing, col_block):
    part = big_product(trailing, col_block)
    return lax.psum_scatter(part, "col", scatter_dimension=0, tiled=True)


def body(
    special,
    trailing,
    factor_one,
    inverse_one,
    factor_two_top,
    factor_two,
    inverse_two,
    structure_one,
    structure_two,
):
    piece_rows = factor_one.shape[0]
    if special and piece_rows == factor_one.shape[1]:
        lists = (structure_one[None, :], structure_two[None, :])
        sums = panels(trailing, factor_one, inverse_one, factor_two, inverse_two, *lists)
        return hand_over(finish(*sums, *lists, inverse_one, inverse_two, factor_two_top))
    row_index = lax.axis_index("row")
    col_index = lax.axis_index("col")
    first_row = (row_index * lax.axis_size("col") + col_index) * piece_rows
    mask_one = block_flags(structure_one, first_row, piece_rows)
    mask_two = block_flags(structure_two, first_row, piece_rows)
    normal_one = mask_one * product(factor_one, inverse_one)
    normal_two = mask_two * product(factor_two, inverse_two)
    normal_top = product(factor_two_top, inverse_two)
    column_one = -mask_one * sweep(trailing, column_panel(normal_one))
    column_two = -mask_two * (sweep(trailing, column_panel(normal_two)) + product(column_one, normal_top))
    parts = (
        product(normal_one.T, column_one),
        product(column_one.T, normal_two),
        product(normal_two.T, column_two),
    )
    first, cross, second = lax.psum(parts, ("row", "col"))
    diagonal_one = product(inverse_one.T, inverse_one) - first
    cross_two = -(product(diagonal_one, normal_top) + cross)
    diagonal_two = product(inverse_two.T, inverse_two) - product(normal_top.T, cross_two) - second
    return (column_one, diagonal_one, column_two, cross_two, diagonal_two)


def solution(mesh):
    special = mesh.shape["row"] == 8 and mesh.shape["col"] == 4
    return jax.shard_map(
        functools.partial(body, special),
        mesh=mesh,
        in_specs=(
            P("row", "col"),
            P(("row", "col"), None),
            P(),
            P(),
            P(("row", "col"), None),
            P(),
            P(),
            P(),
        ),
        out_specs=(P(("row", "col"), None), P(), P(("row", "col"), None), P(), P()),
        check_vma=False,
    )
```

```python
import functools

import jax
import jax.numpy as jnp
from jax import lax
from jax.experimental import pallas as pl
from jax.experimental.pallas import tpu as pltpu
from jax.sharding import PartitionSpec as P

BLK = 128
MESH = pl.DeviceIdType.MESH
CH = 8
AG_LAG = 1
RS_LAG = 5
RS0 = 10
Y0 = 12
NEAR0 = 17
ROOT0 = 37
X_TICK = 8
AG_O, AG_T = (0, 0, 0, 0, 1, 1), (1, 0, 2, 3, 0, 1)
RS_O, RS_T = (1, 0, 0, 0, 0), (0, 3, 0, 2, 1)
B_O, B_T = (1, 1, 0, 1, 0, 1, 0, 0), (1, 0, 0, 3, 3, 2, 2, 1)
A_O, A_T = (0, 0, 0, 0, 1, 1, 1, 1), (1, 0, 2, 3, 0, 2, 3, 1)
Y_T = (3, 1, 2)
QR = CH // 2
AG_N = 2 * len(AG_T) * QR
ROOT_N = 3 * QR
A_TICK = (20, 21, 22, 23, 24, 25, 26, 27, 31, 35, 39, 43, 47, 48, 49, 51)
F32 = jnp.float32
BF16 = jnp.bfloat16


def product(left, right):
    return jnp.dot(left, right, precision=lax.Precision.HIGHEST, preferred_element_type=jnp.float32)


def big_product(left, right):
    return jnp.dot(left, right, precision=lax.Precision.HIGH, preferred_element_type=jnp.float32)


def block_flags(structure, first_row, count):
    blocks = (first_row + jnp.arange(count, dtype=jnp.int32)) // BLK
    hits = jnp.any(blocks[:, None] == structure[None, :], axis=1)
    return hits.astype(jnp.float32)[:, None]


def split(value):
    high = value.astype(BF16)
    return high, (value - high.astype(F32)).astype(BF16)


def mm(left, right):
    return jnp.dot(left, right, preferred_element_type=F32)


def mm3(left, right):
    lh, ll = split(left)
    rh, rl = split(right)
    return mm(lh, rh) + (mm(ll, rh) + mm(lh, rl))


def flip(c, t):
    return ((c // 2 + t // 2) % 2) * 2 + (c % 2 + t % 2) % 2


def pick(table, index):
    return sum(jnp.where(index == i, v, 0) for i, v in enumerate(table) if v)


def row_mask(blocks, piece):
    first = (lax.axis_index("row") * lax.axis_size("col") + lax.axis_index("col")) * piece
    listed = blocks[...]
    rows = first + lax.broadcasted_iota(jnp.int32, (piece, listed.shape[1]), 0)
    hits = jnp.where(rows // BLK == listed, 1.0, 0.0)
    return jnp.max(hits, axis=1, keepdims=True)


def panels_kernel(
    trail, f1, inv1, f2, inv2, list1, list2, y1_out, y2_out, n1_in, n2_in,
    n1buf, n2buf, n2h, n2l, out1, out2, rsu, rsd, rsy, rsn, y2buf, tbuf, n1h, n1l, cbuf, xbuf,
    f_sem, near_sem, ag_sem, n2_sem, up_sem, dn_sem, ry_sem, y2_sem, t_sem, c_sem, x_sem,
    s_up, s_dn, s_y, s_root, s_n2, s_ry, s_line, s_c, s_x,
):
    r, c = lax.axis_index("row"), lax.axis_index("col")
    z, y, x, k = r // 2, r % 2, c // 2, c % 2
    piece = n1_in.shape[0]
    width = n1_in.shape[1]
    cr, gw = piece // QR, width // 2
    wr = n2_in.shape[0] // CH
    ypart = (r + 1 - 2 * y, c)
    cpart = (r, flip(c, 1))
    xpart = (r, flip(c, 2))
    above = (lax.rem(r + 2, 8), c)
    below = (lax.rem(r + 6, 8), c)
    near = jnp.where((z // 2 == x) & (z != c), 1, 0)
    dist = jnp.where(z > c, z - c, c - z)

    def remote(src, dst, send, recv, to):
        return pltpu.make_async_remote_copy(
            src_ref=src, dst_ref=dst, send_sem=send, recv_sem=recv, device_id=to, device_id_type=MESH
        )

    def cols_of(g):
        return pl.ds(pl.multiple_of(g * gw, gw), gw)

    def chunk_of(ch):
        return pl.ds(pl.multiple_of((ch % QR) * cr, cr), cr), cols_of(ch // QR)

    def arrived(ref, sem):
        pltpu.make_async_copy(ref, ref, sem).wait()

    bar = pltpu.get_barrier_semaphore()
    for to in (ypart, cpart, xpart, (r, flip(c, 3))):
        pl.semaphore_signal(bar, inc=1, device_id=to, device_id_type=MESH)

    @pl.when(z < 3)
    def _():
        pl.semaphore_signal(bar, inc=1, device_id=above, device_id_type=MESH)

    @pl.when(z > 0)
    def _():
        pl.semaphore_signal(bar, inc=1, device_id=below, device_id_type=MESH)

    def tile_of(u):
        isa = jnp.where(u >= 16, 1, 0)
        w = (u - 16) * isa
        pb, pa = u % 8, (w // 2) % 8
        t = isa * pick(A_T, pa) + (1 - isa) * pick(B_T, pb)
        o = isa * pick(A_O, pa) + (1 - isa) * pick(B_O, pb)
        h = isa * (w % 2) + (1 - isa) * ((x + u // 8) % 2)
        return ((y + o) % 2) * 4 + flip(c, t), h, t, o

    half = 2 * piece

    def fetch(u):
        j, h, _, _ = tile_of(u)
        rows = pl.ds(pl.multiple_of(h * half, half), half)
        cols = pl.ds(pl.multiple_of(j * piece, piece), piece)
        return pltpu.make_async_copy(trail.at[rows, cols], tbuf.at[u % 2], t_sem.at[u % 2])

    fetch(0).start()
    loads = [pltpu.make_async_copy(a, out2.at[i], f_sem.at[i]) for i, a in enumerate((f2, inv2, f1, inv1))]
    for cp in loads:
        cp.start()
    loads[0].wait()
    loads[1].wait()
    cut = width // 2
    left, right = pl.ds(0, cut), pl.ds(cut, cut)
    listed = row_mask(list2, piece)

    def send_half(rows):
        remote(n2_in.at[rows], n2buf.at[c, rows], s_n2.at[0], n2_sem.at[2], xpart).start()
        remote(n2_in.at[rows], n2buf.at[c, rows], s_n2.at[1], n2_sem.at[1], cpart).start()
        pltpu.make_async_copy(n2_in.at[rows], n2buf.at[c, rows], n2_sem.at[0]).start()

    n2_in[right] = (listed * mm3(out2[0, :, right], out2[1, right, right])).T

    pl.semaphore_wait(bar, 4 + (z + 2) // 3 + (5 - z) // 3)
    send_half(right)
    n2_in[left] = (listed * mm3(out2[0], out2[1, :, left])).T
    send_half(left)

    loads[2].wait()
    loads[3].wait()
    listed = row_mask(list1, piece)
    n1_in[:, left] = listed * mm3(out2[2], out2[3, :, left])
    n1_in[:, right] = listed * mm3(out2[2, :, right], out2[3, right, right])
    here = y * 4 + c
    for ch in range(CH):
        part = chunk_of(ch)

        @pl.when(c == z)
        def _():
            pltpu.make_async_copy(n1_in.at[part], n1buf.at[(here, *part)], ag_sem.at[here, ch]).start()

        @pl.when(c != z)
        def _():
            remote(n1_in.at[part], n1buf.at[(here, *part)], s_root.at[ch], ag_sem.at[here, ch], (r, z)).start()

    arrived(n2buf.at[c], n2_sem.at[0])
    arrived(n2buf.at[flip(c, 1)], n2_sem.at[1])
    for t in range(2):
        q = flip(c, t)
        n2h[q], n2l[q] = split(n2buf[q])

    def ag_of(n):
        g, s, i = n // (len(AG_T) * QR), (n // QR) % len(AG_T), n % QR
        return pick(AG_O, s), pick(AG_T, s), g * QR + i

    def goes_y(o, t):
        return (o == 0) & ((t > 1) | (z == c))

    def ag_step(n):
        o, t, ch = ag_of(n)
        j = ((y + o) % 2) * 4 + flip(c, t)
        chunk = n1buf.at[(j, *chunk_of(ch))]
        arrived(chunk, ag_sem.at[j, ch])

        @pl.when((z >= c) & (z < 3))
        def _():
            remote(chunk, chunk, s_up.at[n], ag_sem.at[j, ch], above).start()

        @pl.when((z <= c) & (z > 0))
        def _():
            remote(chunk, chunk, s_dn.at[n], ag_sem.at[j, ch], below).start()

        @pl.when(goes_y(o, t))
        def _():
            remote(chunk, chunk, s_y.at[t, ch], ag_sem.at[j, ch], ypart).start()

    def rs_step(n):
        s, ch = n // CH, n % CH
        o, t = pick(RS_O, s), pick(RS_T, s)
        j = ((y + o) % 2) * 4 + flip(c, t)
        part = pl.ds(pl.multiple_of(ch * wr, wr), wr)
        chunk = out2.at[j, part]

        @pl.when((z >= c) & (z < 3))
        def _():
            arrived(rsu.at[s, part], up_sem.at[n])
            chunk[...] += rsu[s, part]

        @pl.when((z <= c) & (z > 0))
        def _():
            arrived(rsd.at[s, part], dn_sem.at[n])
            chunk[...] += rsd[s, part]

        @pl.when((o == 0) & ((t > 1) | (z == c) | ((t == 1) & (near == 0))))
        def _():
            arrived(rsy.at[t, part], ry_sem.at[t, ch])
            chunk[...] += rsy[t, part]

        @pl.when(z > c)
        def _():
            remote(chunk, rsu.at[s, part], s_line.at[n], up_sem.at[n], below).start()

        @pl.when(z < c)
        def _():
            remote(chunk, rsd.at[s, part], s_line.at[n], dn_sem.at[n], above).start()

        @pl.when((z == c) & (o == 1))
        def _():
            remote(chunk, rsy.at[0, part], s_line.at[n], ry_sem.at[0, ch], ypart).start()

        @pl.when((z == c) & (o == 0) & (t > 0))
        def _():
            remote(chunk, y2buf.at[part], s_line.at[n], y2_sem.at[ch], (r, flip(c, t))).start()

        @pl.when((z == c) & (o == 0) & (t == 0))
        def _():
            pltpu.make_async_copy(chunk, y2buf.at[part], y2_sem.at[ch]).start()

    def turn_b(u):
        j, h, t, o = tile_of(u)
        fetch(u).wait()
        fetch(u + 1).start()

        @pl.loop(0, 2)
        def _(i):
            rows = pl.ds(pl.multiple_of(i * piece, piece), piece)
            th, tl = split(tbuf[u % 2, rows])
            q = 2 * h + i
            add = mm(n2h[q], th) + (mm(n2l[q], th) + mm(n2h[q], tl))

            @pl.when((u < 8) & (i == 0))
            def _():
                out2[j] = add

            @pl.when((u >= 8) | (i == 1))
            def _():
                out2[j] += add

    def y_step(q):
        t, ch = pick(Y_T, q // CH), q % CH
        part = pl.ds(pl.multiple_of(ch * wr, wr), wr)
        j = ((y + 1) % 2) * 4 + flip(c, t)

        @pl.when((t > 1) | ((near == 0) & (z != c)))
        def _():
            remote(out2.at[j, part], rsy.at[t, part], s_ry.at[t, ch], ry_sem.at[t, ch], ypart).start()

    j_near = ((y + 1) % 2) * 4 + flip(c, 1)

    def near_step(ch):
        part = pl.ds(pl.multiple_of(ch * wr, wr), wr)
        remote(out2.at[j_near, part], rsn.at[part], s_ry.at[1, ch], near_sem.at[ch], (lax.rem(r + jnp.where(z < c, 2, 6), 8), c)).start()

    def root_step(ch):
        part = pl.ds(pl.multiple_of(ch * wr, wr), wr)
        arrived(rsn.at[part], near_sem.at[ch])
        out2[j_near, part] += rsn[part]
        remote(out2.at[j_near, part], rsy.at[1, part], s_ry.at[1, ch], ry_sem.at[1, ch], ypart).start()

    def turn_a(turn):
        g = turn // 8
        cols = cols_of(g)
        j, _, t, o = tile_of(16 + 2 * turn)

        @pl.when((o == 1) & (t >= 2))
        def _():
            for i in range(QR):
                ch = g * QR + i
                arrived(n1buf.at[(j, *chunk_of(ch))], ag_sem.at[j, ch])

        n1h[...], n1l[...] = split(n1buf[j, :, cols])

        @pl.loop(0, 2)
        def _(h):
            u = 16 + 2 * turn + h
            fetch(u).wait()

            @pl.when(u < 47)
            def _():
                fetch(u + 1).start()

            @pl.loop(0, 2)
            def _(i):
                rows = pl.ds(pl.multiple_of(i * piece, piece), piece)
                th, tl = split(tbuf[u % 2, rows])
                add = mm(th, n1h[...]) + (mm(th, n1l[...]) + mm(tl, n1h[...]))
                q = 2 * h + i

                @pl.when(turn % 8 == 0)
                def _():
                    out1[q, :, cols] = add

                @pl.when(turn % 8 > 0)
                def _():
                    out1[q, :, cols] += add

    qx = flip(c, 2)
    ag_first = AG_LAG * dist
    rs_first = RS0 + RS_LAG * jnp.where(z > c, 3 - z, jnp.where(z < c, z, jnp.where(c < 2, 3 - c, c)))

    def core_copy(g, i):
        to = flip(c, 1 + 2 * (1 - i))
        cols = cols_of(g)
        return remote(out1.at[to, :, cols], cbuf.at[i, :, cols], s_c.at[g, i], c_sem.at[g, i], cpart)

    def x_copy(g):
        cols = cols_of(g)
        return remote(out1.at[qx, :, cols], xbuf.at[:, cols], s_x.at[g], x_sem.at[g], xpart)

    def tick(step, carry):
        two = jnp.where((z == c) & (step >= ROOT_N), 1, 0)

        @pl.loop(0, 1 + two)
        def _(i):
            n = jnp.where(two == 1, ROOT_N + (step - ROOT_N) * 2 + i, step - ag_first)

            @pl.when((n >= 0) & (n < AG_N))
            def _():
                ag_step(n)

        m = step - rs_first

        @pl.when((m >= 0) & (m < 5 * CH))
        def _():
            rs_step(m)

        @pl.when(step == X_TICK)
        def _():
            got = flip(c, 2)
            arrived(n2buf.at[got], n2_sem.at[2])
            fwd = remote(n2buf.at[got], n2buf.at[got], s_n2.at[2], n2_sem.at[3], cpart)
            fwd.start()
            n2h[got], n2l[got] = split(n2buf[got])
            last = flip(c, 3)
            arrived(n2buf.at[last], n2_sem.at[3])
            n2h[last], n2l[last] = split(n2buf[last])

        @pl.when(step < 16)
        def _():
            turn_b(step)

        for i in range(2):
            e = (step - NEAR0) * 2 + i

            @pl.when((near == 1) & (e >= 0) & (e < CH))
            def _():
                near_step(e)

        e = step - ROOT0

        @pl.when((z == c) & (e >= 0) & (e < CH))
        def _():
            root_step(e)

        q = step - Y0

        @pl.when((q >= 0) & (q < 3 * CH))
        def _():
            y_step(q)

        @pl.when(sum(jnp.where(step == a, 1, 0) for a in A_TICK) > 0)
        def _():
            turn_a(sum(jnp.where(step >= a, 1, 0) for a in A_TICK) - 1)

        for g in range(2):
            end_a = A_TICK[8 * g + 7] + 1

            @pl.when(step == end_a)
            def _():
                core_copy(g, 0).start()
                core_copy(g, 1).start()

            @pl.when(step == end_a + 1)
            def _():
                cols = cols_of(g)
                core_copy(g, 0).wait_recv()
                out1[qx, :, cols] += cbuf[0, :, cols]
                x_copy(g).start()
                core_copy(g, 1).wait_recv()
                out1[c, :, cols] += cbuf[1, :, cols]

        return carry

    last_tick = max(RS0 + 3 * RS_LAG + 5 * CH, AG_N + 3 * AG_LAG, A_TICK[15] + 3, Y0 + 3 * CH)
    lax.fori_loop(0, last_tick, tick, 0)

    for g in range(2):
        x_copy(g).wait_recv()
    y1_out[...] = out1[c] + xbuf[...]
    for ch in range(CH):
        part = pl.ds(ch * wr, wr)
        arrived(y2buf.at[part], y2_sem.at[ch])
    y2_out[...] = y2buf[...]

    def sent(ref, sem):
        pltpu.make_async_copy(ref, ref, sem).wait()

    whole = n2buf.at[0]
    for i in range(3):
        sent(whole, s_n2.at[i])
    for g in range(2):
        for i in range(2):
            core_copy(g, i).wait_send()
        x_copy(g).wait_send()
    bit = n1buf.at[(0, *chunk_of(0))]
    wbit = out2.at[0, pl.ds(0, wr)]

    @pl.loop(0, AG_N)
    def _(n):
        o, t, ch = ag_of(n)

        @pl.when((z >= c) & (z < 3))
        def _():
            sent(bit, s_up.at[n])

        @pl.when((z <= c) & (z > 0))
        def _():
            sent(bit, s_dn.at[n])

        @pl.when(goes_y(o, t))
        def _():
            sent(bit, s_y.at[t, ch])

    @pl.loop(0, 5 * CH)
    def _(n):
        s, ch = n // CH, n % CH

        @pl.when((z != c) | (pick(RS_O, s) == 1) | (pick(RS_T, s) > 0))
        def _():
            sent(wbit, s_line.at[n])

        @pl.when(s < 3)
        def _():
            sent(wbit, s_ry.at[s + 1, ch])

        @pl.when((s == 0) & (c != z))
        def _():
            sent(bit, s_root.at[ch])


def panels(trailing, f1, inv1, f2, inv2, list1, list2):
    piece, width = f1.shape
    dma = pltpu.SemaphoreType.DMA
    vm = pltpu.VMEM
    scratch = [
        vm((8, piece, width), F32),
        vm((4, width, piece), F32),
        vm((4, width, piece), BF16),
        vm((4, width, piece), BF16),
        vm((4, piece, width), F32),
        vm((8, width, piece), F32),
        vm((5, width, piece), F32),
        vm((5, width, piece), F32),
        vm((4, width, piece), F32),
        vm((width, piece), F32),
        vm((width, piece), F32),
        vm((2, 2 * piece, piece), F32),
        vm((piece, width // 2), BF16),
        vm((piece, width // 2), BF16),
        vm((2, piece, width), F32),
        vm((piece, width), F32),
        dma((4,)), dma((CH,)), dma((8, CH)), dma((4,)), dma((5 * CH,)), dma((5 * CH,)), dma((4, CH)), dma((CH,)), dma((2,)), dma((2, 2)), dma((2,)),
        dma((AG_N,)), dma((AG_N,)), dma((4, CH)), dma((CH,)), dma((3,)), dma((4, CH)), dma((5 * CH,)), dma((2, 2)), dma((2,)),
    ]
    anyspace = pl.BlockSpec(memory_space=pl.ANY)
    inv = pl.BlockSpec(memory_space=pltpu.VMEM)
    return pl.pallas_call(
        panels_kernel,
        out_shape=(
            jax.ShapeDtypeStruct((piece, width), F32),
            jax.ShapeDtypeStruct((width, piece), F32),
        )
        * 2,
        in_specs=[anyspace] * 5 + [inv, inv],
        out_specs=(inv,) * 4,
        scratch_shapes=scratch,
        compiler_params=pltpu.CompilerParams(
            collective_id=0, has_side_effects=True, vmem_limit_bytes=63 * 2**20
        ),
        name="panels",
    )(trailing, f1, inv1, f2, inv2, list1, list2)


def finish_kernel(
    y1, y2t, n1, n2t, list1, list2, inv1, inv2, f_top,
    col1, diag1, col2, cross2, diag2,
    part0, part1, part2, sum0, sum1, sum2, top, top_t, square1, square2,
    acc, got1, got2, got3, got4, recv, send, z_recv, z_send, z_back, z_out,
):
    parts, outs = (part0, part1, part2), (sum0, sum1, sum2)
    r, c = lax.axis_index("row"), lax.axis_index("col")
    z, y, x, k = r // 2, r % 2, c // 2, c % 2
    ypart = (r + 1 - 2 * y, c)
    cpart = (r, flip(c, 1))
    xpart = (r, flip(c, 2))
    rows, cols = part1.shape
    half, quarter = rows // 2, rows // 4
    zw = cols // 4
    first, second = (x, y), (y, x)
    one, two = (xpart, ypart), (ypart, xpart)
    h1, h2, h3 = ([parts[m].shape[0] // d for m in range(3)] for d in (2, 8, 16))
    base = [k * h1[m] for m in range(3)]
    at1 = [[i * (h1[m] // 2) + first[i] * h2[m] for i in (0, 1)] for m in range(3)]
    at2 = [[at1[m][i] + second[i] * h3[m] for i in (0, 1)] for m in range(3)]
    line = [(lax.rem(r + 2 * d, 8), c) for d in (1, 2, 3)]

    def remote(src, dst, s_sem, r_sem, to):
        return pltpu.make_async_remote_copy(
            src_ref=src, dst_ref=dst, send_sem=s_sem, recv_sem=r_sem, device_id=to, device_id_type=MESH
        )

    def span(start, size):
        return pl.ds(pl.multiple_of(start, 8), size)

    def side(zz):
        return pl.ds(pl.multiple_of(zz * zw, zw), zw)

    bar = pltpu.get_barrier_semaphore()
    for to in [ypart, cpart, xpart] + line:
        pl.semaphore_signal(bar, inc=1, device_id=to, device_id_type=MESH)
    pl.semaphore_wait(bar, 6)

    def copies(m, stage):
        if stage == 0:
            there = parts[m].at[span((1 - k) * h1[m], h1[m])]
            return [remote(there, got1.at[m, span(0, h1[m])], send.at[m, 0, 0], recv.at[m, 0, 0], cpart)]
        if stage == 1:
            return [
                remote(
                    acc.at[m, span(i * (h1[m] // 2) + (1 - first[i]) * h2[m], h2[m])],
                    got2.at[m, i, span(0, h2[m])], send.at[m, 1, i], recv.at[m, 1, i], one[i],
                )
                for i in (0, 1)
            ]
        if stage == 2:
            return [
                remote(
                    acc.at[m, span(at1[m][i] + (1 - second[i]) * h3[m], h3[m])],
                    got3.at[m, i, span(0, h3[m])], send.at[m, 2, i], recv.at[m, 2, i], two[i],
                )
                for i in (0, 1)
            ]
        if stage == 3:
            return [
                remote(
                    acc.at[m, span(at2[m][i], h3[m]), side(lax.rem(z + d, 4))],
                    got4.at[m, d - 1, i, span(0, h3[m])], z_send.at[m, d - 1, i], z_recv.at[m, d - 1, i], line[d - 1],
                )
                for d in (1, 2, 3)
                for i in (0, 1)
            ]
        if stage == 4:
            places = [outs[m].at[span(base[m] + at2[m][i], h3[m]), side(z)] for i in (0, 1)]
            return [
                remote(places[i], places[i], z_out.at[m, d - 1, i], z_back.at[m, d - 1, i], line[d - 1])
                for d in (1, 2, 3)
                for i in (0, 1)
            ]
        if stage == 7:
            place = outs[m].at[span(base[m], h1[m])]
            return [remote(place, place, send.at[m, 5, 0], recv.at[m, 5, 0], cpart)]
        to = (two, one)[stage - 5]
        size, at = ((h3[m], at2[m]), (h2[m], at1[m]))[stage - 5]
        places = [outs[m].at[span(base[m] + at[i], size)] for i in (0, 1)]
        return [remote(places[i], places[i], send.at[m, stage - 2, i], recv.at[m, stage - 2, i], to[i]) for i in (0, 1)]

    def take(m, stage):
        for cp in copies(m, stage):
            cp.wait_recv()
        if stage == 0:
            acc[m, span(0, h1[m])] = parts[m][span(base[m], h1[m])] + got1[m, span(0, h1[m])]
        for i in (0, 1):
            if stage == 1:
                acc[m, span(at1[m][i], h2[m])] += got2[m, i, span(0, h2[m])]
            if stage == 2:
                acc[m, span(at2[m][i], h3[m])] += got3[m, i, span(0, h3[m])]
            if stage == 3:
                got = [got4[m, d, i, span(0, h3[m])] for d in range(3)]
                mine = acc[m, span(at2[m][i], h3[m]), side(z)] + got[0] + (got[1] + got[2])
                outs[m][span(base[m] + at2[m][i], h3[m]), side(z)] = mine

    def pack(part, left, right):
        part[0:half] = mm3(left[0:half], right)
        last = mm3(left[half:rows], right[:, half:cols])
        part[half : half + quarter, 0:half] = last[0:quarter]
        part[half : half + quarter, half:cols] = last[quarter:half]

    def minus(out, value, total):
        out[0:half] = value[0:half] - total[0:half]
        out[half:rows, 0:half] = value[half:rows, 0:half] - total[0:half, half:cols].T
        out[half : half + quarter, half:cols] = value[half : half + quarter, half:cols] - total[half : half + quarter, 0:half]
        out[half + quarter : rows, half:cols] = value[half + quarter : rows, half:cols] - total[half : half + quarter, half:cols]

    def make(m):
        if m == 0:
            col1[...] = -row_mask(list1, rows) * y1[...]
            pack(part0, n1[...].T, col1[...])
        if m == 1:
            part1[...] = mm3(n2t[...], col1[...])
        if m == 2:
            col2[...] = -row_mask(list2, rows) * y2t[...].T
            pack(part2, n2t[...], col2[...])

    for step in range(8 + 3):
        if step == 3:
            top[...] = mm3(f_top[...], inv2[...])
            square1[...] = mm3(inv1[...].T, inv1[...])
        if step == 4:
            square2[...] = mm3(inv2[...].T, inv2[...])
        if step == 5:
            top_t[...] = top[...].T
        if step == 6:
            col2[...] -= row_mask(list2, rows) * mm3(col1[...], top[...])
        for m in range(3):
            stage = step - m
            if stage == 0:
                make(m)
            if 1 <= stage <= 8:
                take(m, stage - 1)
            if 0 <= stage < 8:
                for cp in copies(m, stage):
                    cp.start()
        if step == 9:
            minus(diag1, square1, sum0)
            cross2[...] = -(mm3(diag1[...], top[...]) + sum1[...].T)
            square2[...] += mm3(sum1[...], top[...]) - mm3(top_t[...], cross2[...])
    minus(diag2, square2, sum2)
    for m in range(3):
        for stage in range(8):
            for cp in copies(m, stage):
                cp.wait_send()


def finish(y1, y2t, n1, n2t, list1, list2, inv1, inv2, f_top):
    rows, cols = y1.shape
    dma = pltpu.SemaphoreType.DMA
    vm = pltpu.VMEM
    inv = pl.BlockSpec(memory_space=pltpu.VMEM)
    return pl.pallas_call(
        finish_kernel,
        out_shape=(jax.ShapeDtypeStruct((rows, cols), F32),) * 5,
        in_specs=[inv] * 9,
        out_specs=(inv,) * 5,
        scratch_shapes=[
            vm((3 * rows // 4, cols), F32), vm((rows, cols), F32), vm((3 * rows // 4, cols), F32),
            vm((3 * rows // 4, cols), F32), vm((rows, cols), F32), vm((3 * rows // 4, cols), F32),
            *[vm((rows, cols), F32)] * 4,
            vm((3, rows // 2, cols), F32),
            vm((3, rows // 2, cols), F32),
            vm((3, 2, rows // 8, cols), F32),
            vm((3, 2, rows // 16, cols), F32),
            vm((3, 3, 2, rows // 16, cols // 4), F32),
            dma((3, 6, 2)), dma((3, 6, 2)),
            dma((3, 3, 2)), dma((3, 3, 2)), dma((3, 3, 2)), dma((3, 3, 2)),
        ],
        compiler_params=pltpu.CompilerParams(
            collective_id=1, has_side_effects=True, vmem_limit_bytes=60 * 2**20
        ),
        name="finish",
    )(y1, y2t, n1, n2t, list1, list2, inv1, inv2, f_top)


def hand_over_kernel(*refs):
    for i in range(5):
        refs[5 + i][...] = refs[i][...]


def hand_over(arrays):
    inv = pl.BlockSpec(memory_space=pltpu.VMEM)
    return pl.pallas_call(
        hand_over_kernel,
        out_shape=tuple(jax.ShapeDtypeStruct(a.shape, a.dtype) for a in arrays),
        in_specs=[inv] * 5,
        out_specs=(inv,) * 5,
        name="hand_over",
    )(*arrays)


def column_panel(normal):
    rows, cols = lax.axis_size("row"), lax.axis_size("col")
    moves = [(p, (p % rows) * cols + p // rows) for p in range(rows * cols)]
    piece = lax.ppermute(normal, ("row", "col"), moves)
    return lax.all_gather(piece, "row", axis=0, tiled=True)


def sweep(trailing, col_block):
    part = big_product(trailing, col_block)
    return lax.psum_scatter(part, "col", scatter_dimension=0, tiled=True)


def body(
    special,
    trailing,
    factor_one,
    inverse_one,
    factor_two_top,
    factor_two,
    inverse_two,
    structure_one,
    structure_two,
):
    piece_rows = factor_one.shape[0]
    if special and piece_rows == factor_one.shape[1]:
        lists = (structure_one[None, :], structure_two[None, :])
        sums = panels(trailing, factor_one, inverse_one, factor_two, inverse_two, *lists)
        return hand_over(finish(*sums, *lists, inverse_one, inverse_two, factor_two_top))
    row_index = lax.axis_index("row")
    col_index = lax.axis_index("col")
    first_row = (row_index * lax.axis_size("col") + col_index) * piece_rows
    mask_one = block_flags(structure_one, first_row, piece_rows)
    mask_two = block_flags(structure_two, first_row, piece_rows)
    normal_one = mask_one * product(factor_one, inverse_one)
    normal_two = mask_two * product(factor_two, inverse_two)
    normal_top = product(factor_two_top, inverse_two)
    column_one = -mask_one * sweep(trailing, column_panel(normal_one))
    column_two = -mask_two * (sweep(trailing, column_panel(normal_two)) + product(column_one, normal_top))
    parts = (
        product(normal_one.T, column_one),
        product(column_one.T, normal_two),
        product(normal_two.T, column_two),
    )
    first, cross, second = lax.psum(parts, ("row", "col"))
    diagonal_one = product(inverse_one.T, inverse_one) - first
    cross_two = -(product(diagonal_one, normal_top) + cross)
    diagonal_two = product(inverse_two.T, inverse_two) - product(normal_top.T, cross_two) - second
    return (column_one, diagonal_one, column_two, cross_two, diagonal_two)


def solution(mesh):
    special = mesh.shape["row"] == 8 and mesh.shape["col"] == 4
    return jax.shard_map(
        functools.partial(body, special),
        mesh=mesh,
        in_specs=(
            P("row", "col"),
            P(("row", "col"), None),
            P(),
            P(),
            P(("row", "col"), None),
            P(),
            P(),
            P(),
        ),
        out_specs=(P(("row", "col"), None), P(), P(("row", "col"), None), P(), P()),
        check_vma=False,
    )
```
